128 devices in a mesh: gx: 8 (over y, x_hi), gy: 16 (over z, x_lo, core).
Axes of the slice: x: 4 (x_hi: 2, x_lo: 2; x = x_hi * 2 + x_lo), y: 4, z: 4, core: 2. Of those that a mesh axis runs over, the one named last changes fastest.
Arguments:
- displacement: float32 [3, 128, 256, 128], P(None, 'gy', 'gx'), may hold values from -0.25 to 0.25
- volume: float32 [128, 256, 128], P('gy', 'gx'), may hold values from 0.5 to 2
- material: int32 [128, 256], P('gy', 'gx'), may hold values from 0 to 1, as said below
- layers: int32 [128, 256], P('gy', 'gx'), may hold values from 126 to 128
Outputs:
- factors: float32 [3, 128, 256, 128], P(None, 'gy', 'gx')
- force: float32 [3, 128, 256, 128], P(None, 'gy', 'gx')
The draws below stay inside these ranges and needn't reach their ends.
Inputs may be any that keep to these rules, and one draw needn't show every extreme that they name: `material`: A slit two rows wide, cut from the plate's edge x = 0 into the plate, is 0, and scattered further columns are 0; all others are 1.
All inputs are finite; a program needn't handle non-finite values.
Results may differ from the reference program's by a relative error of at most 0.0003.
Values sent between devices are 32-bit elements; how exact they have to be, the bound alone decides.
A program may use at most 128 MiB of HBM per device.

```python
import math
import jax
import jax.numpy as jnp
import numpy as np
from jax import lax

HORIZON = 3
NZ = 128
NY = 128
NX = 256


def draw_material(key, part):
    key_rows, key_tip, key_missing = jax.random.split(key, 3)
    row_start = jax.random.randint(key_rows, (), NY // 4, 3 * NY // 4)
    tip_column = jax.random.randint(key_tip, (), NX // 4, 3 * NX // 4 + 1)
    row_index = jnp.arange(NY, dtype=jnp.int32)[:, None]
    column_index = jnp.arange(NX, dtype=jnp.int32)[None, :]
    slit_cells = (row_index >= row_start) & (row_index < row_start + 2) & (column_index < tip_column)
    missing = jax.random.randint(key_missing, (NY, NX), 0, 32) == 0
    return jnp.where(slit_cells | missing, 0, 1).astype(jnp.int32)


def set_ends(values, stream_key, least, high):
    index_at = [jax.random.randint(jax.random.fold_in(stream_key, axis), (), 0, length) for axis, length in enumerate(values.shape)]
    main_axis = values.shape.index(max(values.shape))
    neighbour = index_at[:main_axis] + [(index_at[main_axis] + 1) % values.shape[main_axis]] + index_at[main_axis + 1:]
    return values.at[tuple(index_at)].set(least).at[tuple(neighbour)].set(high)


def levels(rng, extent, pieces, smallest, high):
    def one(axis_at, parts):
        draws = jax.random.uniform(jax.random.fold_in(jax.random.fold_in(rng, 6), axis_at), (parts,), jnp.float32, smallest / len(pieces), high / len(pieces))
        return jnp.repeat(jnp.exp(draws), extent[axis_at] // parts).reshape((-1,) + (1,) * (len(extent) - axis_at - 1))

    level = one(*pieces[0])
    for cut in pieces[1:]:
        level = level * one(*cut)
    return level


def gaussian(key, shape, scale, most, shards=(), held_as=jnp.bfloat16):
    loudness = levels(key, shape, shards, -0.22, 0.18) if shards else 1.0
    drawn = jax.random.normal(key, shape, jnp.float32) * scale * loudness
    return jnp.minimum(jnp.maximum(drawn, -most), most).astype(held_as)


def setup_inputs(seed: int = 0) -> dict:
    seeds = jax.random.split(jax.random.key(seed), 5)
    return {
        "displacement": gaussian(seeds[0], (3, NY, NX, NZ), 0.08, 0.25, ((1, 16), (2, 8)), jnp.float32),
        "volume": jnp.clip(jnp.exp(math.log(2.0) - 1.3862944 * jax.random.uniform(seeds[1], (NY, NX, NZ), jnp.float32) ** levels(seeds[1], (NY, NX, NZ), ((0, 16), (1, 8)), -0.2, 0.2)), 0.5, 2.0),
        "material": draw_material(jax.random.fold_in(seeds[4], 71), 0),
        "layers": set_ends(jax.random.randint(seeds[3], (NY, NX), NZ - 2, NZ + 1), jax.random.fold_in(seeds[3], 1), NZ - 2, NZ).astype(jnp.int32),
    }


STIFF = 5.0

def bond_list():
    bond_set = []
    for step_y in range(-HORIZON, HORIZON + 1):
        for step_x in range(-HORIZON, HORIZON + 1):
            for step_z in range(-HORIZON, HORIZON + 1):
                square_dist = step_x * step_x + step_y * step_y + step_z * step_z
                if 0 < square_dist <= HORIZON * HORIZON:
                    bond_set.append((step_x, step_y, step_z))
    return bond_set

def bond_table():
    offsets = []
    weights = []
    for step_x, step_y, step_z in bond_list():
        square_dist = step_x * step_x + step_y * step_y + step_z * step_z
        length = math.sqrt(square_dist)
        influence = (1.0 - square_dist / (HORIZON * HORIZON)) ** 2
        energy_parts = [influence * component ** 4 / length ** 3 for component in (step_x, step_y, step_z)]
        offsets.append([step_x, step_y, step_z])
        weights.append([length, influence] + energy_parts)
    return (jnp.asarray(np.array(offsets, np.int32)), jnp.asarray(np.array(weights, np.float32)))

def alive_of(material, layers, depth):
    layer_index = jnp.arange(depth, dtype=jnp.int32)
    filled = (material[:, :, None] > 0) & (layer_index[None, None, :] < layers[:, :, None])
    return jnp.where(filled, 1.0, 0.0).astype(jnp.float32)

def padded(field):
    return jnp.pad(field, ((0, 0), (HORIZON, HORIZON), (HORIZON, HORIZON), (HORIZON, HORIZON)))

def take(field_pad, offset, grid_rows, grid_columns, depth):
    starts = (jnp.int32(0), (HORIZON + offset[1]).astype(jnp.int32), (HORIZON + offset[0]).astype(jnp.int32), (HORIZON + offset[2]).astype(jnp.int32))
    return lax.dynamic_slice(field_pad, starts, (field_pad.shape[0], grid_rows, grid_columns, depth))

def reference(displacement, volume, material, layers):
    grid_rows, grid_columns, depth = volume.shape
    alive = alive_of(material, layers, depth)
    vol_live = (volume * alive)[None]
    vol_pad = padded(vol_live)
    disp_pad = padded(displacement)
    offsets, weights = bond_table()

    def energy_step(energy, item):
        offset, weight = item
        nearby = take(vol_pad, offset, grid_rows, grid_columns, depth)
        return (energy + weight[2:5][:, None, None, None] * nearby, None)
    energy, _ = lax.scan(energy_step, jnp.zeros((3, grid_rows, grid_columns, depth), jnp.float32), (offsets, weights))
    bulk_energy = math.pi * HORIZON ** 4 / 30.0
    safe_energy = jnp.where(alive[None] > 0, energy, 1.0)
    factors = jnp.where(alive[None] > 0, bulk_energy / safe_energy, 1.0).astype(jnp.float32)
    fac_pad = padded(factors)

    def force_step(force, item):
        offset, weight = item
        length = weight[0]
        influence = weight[1]
        nearby_disp = take(disp_pad, offset, grid_rows, grid_columns, depth)
        nearby_fac = take(fac_pad, offset, grid_rows, grid_columns, depth)
        nearby_vol = take(vol_pad, offset, grid_rows, grid_columns, depth)
        step = offset.astype(jnp.float32)[:, None, None, None]
        stretched = step + nearby_disp - displacement
        current = jnp.sqrt(lax.optimization_barrier(jnp.sum(stretched * stretched, axis=0, keepdims=True)))
        mean_factor = 0.5 * (factors + nearby_fac)
        inverse = lax.optimization_barrier(jnp.sum((step / length / mean_factor) ** 2, axis=0, keepdims=True))
        stretch = current / length - 1.0
        pull = STIFF * influence * lax.rsqrt(inverse) * stretch / current * stretched
        return (force + pull * nearby_vol, None)
    force, _ = lax.scan(force_step, jnp.zeros((3, grid_rows, grid_columns, depth), jnp.float32), (offsets, weights))
    force = force * alive[None]
    return (factors, force)
```

```python
import functools
import math

import jax
import jax.numpy as jnp
from jax import lax
from jax.experimental import pallas as pl
from jax.experimental.pallas import tpu as pltpu
from jax.sharding import PartitionSpec as P

HORIZON = 3
STIFF = 5.0
WIDE = 2 * HORIZON
LANES = 128
SUB = 8
MESH = pl.DeviceIdType.MESH
SIDES = (-1, 1)
STEPS = tuple((dx, dy) for dy in (-1, 0, 1) for dx in (-1, 0, 1) if (dx, dy) != (0, 0))
CORNERS = tuple(step for step in STEPS if step[0] and step[1])


def bond_list():
    reach = range(-HORIZON, HORIZON + 1)
    return [
        (x, y, z)
        for y in reach
        for x in reach
        for z in reach
        if 0 < x * x + y * y + z * z <= HORIZON * HORIZON
    ]


def bond_types():
    kinds = {}
    for bond in bond_list():
        kinds.setdefault(tuple(sorted(map(abs, bond))), []).append(bond)
    return kinds


def influence(square):
    return (1.0 - square / (HORIZON * HORIZON)) ** 2


def pair_list():
    reach = range(HORIZON + 1)
    return [(ax, az) for ax in reach for az in reach if ax * ax + az * az <= HORIZON * HORIZON]


TPAIRS = [pair for pair in pair_list() if pair[0] > 0]


def shifted(value, step):
    return pltpu.roll(value, (-step) % LANES, 1) if step else value


def kernel(
    disp, volume, material, layers, fac_out, force_out,
    vol_ext, mirror, mirror_x, ext, send_x, send_c, got_y, got_x, got_c, sems,
):
    rows, cols = volume.shape[0], volume.shape[1]
    left = SUB
    gx, gy = lax.axis_index("gx"), lax.axis_index("gy")
    nx, ny = lax.axis_size("gx"), lax.axis_size("gy")

    def has(step):
        dx, dy = step
        found = None
        for delta, at, size in ((dx, gx, nx), (dy, gy, ny)):
            if delta:
                test = at > 0 if delta < 0 else at < size - 1
                found = test if found is None else found & test
        return found

    def device(step):
        return {"gx": gx + step[0], "gy": gy + step[1]}

    barrier = pltpu.get_barrier_semaphore()
    for step in STEPS:

        @pl.when(has(step))
        def _():
            pl.semaphore_signal(barrier, inc=1, device_id=device(step), device_id_type=MESH)

    lane = lax.broadcasted_iota(jnp.int32, (SUB, LANES), 1)
    sub = lax.broadcasted_iota(jnp.int32, (SUB, LANES), 0)
    sub_f = sub.astype(jnp.float32)
    zero = jnp.zeros((SUB, LANES), jnp.float32)

    eye_row = lax.broadcasted_iota(jnp.int32, (cols, cols), 0)
    eye_col = lax.broadcasted_iota(jnp.int32, (cols, cols), 1)
    level = lax.broadcasted_iota(jnp.int32, (cols, LANES), 1).astype(jnp.float32)
    filled = jnp.where(material[...] > 0, layers[...], 0).astype(jnp.float32)
    for y in range(rows):
        line = jnp.broadcast_to(filled[y : y + 1, :], (cols, cols))
        top = jnp.sum(jnp.where(eye_row == eye_col, line, 0.0), axis=1, keepdims=True)
        vol_ext[WIDE + y, left : left + cols, :] = jnp.where(
            level < jnp.broadcast_to(top, (cols, LANES)), volume[y], 0.0
        )

    for side, first in ((0, 0), (1, cols - HORIZON)):
        for k in range(3):
            for y in range(rows):
                at = (k * rows + y) * HORIZON
                send_x[side, at : at + HORIZON, :] = disp[k, y, first : first + HORIZON, :]
    for index, (dx, dy) in enumerate(CORNERS):
        first = 0 if dx < 0 else cols - HORIZON
        start = 0 if dy < 0 else rows - HORIZON
        for k in range(3):
            for y in range(HORIZON):
                at = (k * HORIZON + y) * HORIZON
                send_c[index, at : at + HORIZON, :] = disp[k, start + y, first : first + HORIZON, :]

    right = left + cols
    bottom = WIDE + rows

    def clear(ref, *where):
        ref[where] = jnp.zeros(ref.at[where].shape, jnp.float32)

    @pl.when(gx == 0)
    def _():
        clear(vol_ext, slice(None), slice(0, left))
        clear(got_x, 0)

    @pl.when(gx == nx - 1)
    def _():
        clear(vol_ext, slice(None), slice(right, right + SUB))
        clear(got_x, 1)

    @pl.when(gy == 0)
    def _():
        clear(vol_ext, slice(0, WIDE))
        clear(got_y, 0)

    @pl.when(gy == ny - 1)
    def _():
        clear(vol_ext, slice(bottom, bottom + WIDE))
        clear(got_y, 1)

    for index, step in enumerate(CORNERS):

        @pl.when(jnp.logical_not(has(step)))
        def _():
            clear(got_c, index)

    peers = sum(has(step).astype(jnp.int32) for step in STEPS)
    pl.semaphore_wait(barrier, peers)

    def cut_from(delta, size, width):
        return {-1: (0, width), 0: (0, size), 1: (size - width, width)}[delta]

    def vol_copy(step):
        dx, dy = step
        y0, yn = cut_from(dy, rows, WIDE)
        x0, xn = cut_from(dx, cols, SUB)
        to_y = {-1: bottom, 0: WIDE, 1: 0}[dy]
        to_x = {-1: right, 0: left, 1: 0}[dx]
        slot = STEPS.index(step)
        return pltpu.make_async_remote_copy(
            src_ref=vol_ext.at[WIDE + y0 : WIDE + y0 + yn, left + x0 : left + x0 + xn],
            dst_ref=vol_ext.at[to_y : to_y + yn, to_x : to_x + xn],
            send_sem=sems.at[0, slot],
            recv_sem=sems.at[1, STEPS.index((-dx, -dy))],
            device_id=device(step),
            device_id_type=MESH,
        )

    def disp_copy(step):
        dx, dy = step
        slot = STEPS.index(step)
        if dx == 0:
            y0, yn = cut_from(dy, rows, HORIZON)
            source, target = disp.at[:, y0 : y0 + yn], got_y.at[0 if dy > 0 else 1]
        elif dy == 0:
            source, target = send_x.at[0 if dx < 0 else 1], got_x.at[0 if dx > 0 else 1]
        else:
            source, target = send_c.at[CORNERS.index(step)], got_c.at[CORNERS.index((-dx, -dy))]
        return pltpu.make_async_remote_copy(
            src_ref=source,
            dst_ref=target,
            send_sem=sems.at[2, slot],
            recv_sem=sems.at[3, STEPS.index((-dx, -dy))],
            device_id=device(step),
            device_id_type=MESH,
        )

    order = sorted(STEPS, key=lambda step: (-abs(step[0]) - abs(step[1]), -abs(step[0])))
    for make in (vol_copy, disp_copy):
        for step in order:

            @pl.when(has(step))
            def _():
                make(step).start()

    def arrived(make, step):
        @pl.when(has(step))
        def _():
            dx, dy = step
            make((-dx, -dy)).wait_recv()

    def put(k, y, at, value):
        width = value.shape[0]
        for oz in range(-2, 3):
            moved = shifted(value, oz)
            if k == 2 and oz:
                moved = moved + float(oz)
            ext[k * 5 + oz + 2, y, pl.ds(at, width), :] = moved

    middle_x = left + cols // 2
    middle_y = HORIZON + rows // 2

    def position(k, value, y, at):
        if k == 0:
            index = sub_f[: value.shape[0]] if value.shape[0] < SUB else sub_f
            return value + (index + float(at - middle_x))
        if k == 1:
            return value + (y - middle_y).astype(jnp.float32)
        return value

    def own_row(y, carry):
        for k in range(3):
            for at in range(0, cols, SUB):
                value = position(k, disp[k, y, at : at + SUB, :], y + HORIZON, left + at)
                put(k, y + HORIZON, left + at, value)
        return carry

    lax.fori_loop(0, rows, own_row, 0)

    for step in order:
        arrived(vol_copy, step)

    def mirror_row(r, carry):
        for at in range(0, right + SUB, SUB):
            value = vol_ext[r, at : at + SUB, :]
            parts = []
            for a in range(1, HORIZON + 1):
                ahead = jnp.where(lane < LANES - a, shifted(value, a), 0.0)
                behind = jnp.where(lane >= a, shifted(value, -a), 0.0)
                mirror[a - 1, r, at : at + SUB, :] = ahead + behind
                parts.append((ahead, behind))

            @pl.when((r >= HORIZON) & (r < HORIZON + ext.shape[1]))
            def _():
                ext[6 * 5 + 2, r - HORIZON, at : at + SUB, :] = value
                for a in (1, 2):
                    ext[6 * 5 + 2 + a, r - HORIZON, at : at + SUB, :] = parts[a - 1][0]
                    ext[6 * 5 + 2 - a, r - HORIZON, at : at + SUB, :] = parts[a - 1][1]

        for tile in range(mirror_x.shape[2] // SUB):
            at = left - HORIZON + tile * SUB
            for index, (ax, az) in enumerate(TPAIRS):
                total = side_sum(az, r, at + ax) + side_sum(az, r, at - ax)
                mirror_x[index, r, tile * SUB : tile * SUB + SUB, :] = total
        return carry

    def side_sum(az, r, at):
        if az == 0:
            return vol_ext[r, at : at + SUB, :]
        return mirror[az - 1, r, at : at + SUB, :]

    lax.fori_loop(0, vol_ext.shape[0], mirror_row, 0)

    bulk = math.pi * HORIZON**4 / 30.0

    def factor_row(y, carry):
        r = y + HORIZON
        for tile in range(mirror_x.shape[2] // SUB):
            at = left - HORIZON + tile * SUB

            def pick(ax, az, row):
                if ax:
                    return mirror_x[TPAIRS.index((ax, az)), row, tile * SUB : tile * SUB + SUB, :]
                return side_sum(az, row, at)

            energy = [zero, zero, zero]
            for ax, az in pair_list():
                for ay in range(HORIZON + 1):
                    square = ax * ax + ay * ay + az * az
                    if not 0 < square <= HORIZON * HORIZON:
                        continue
                    total = pick(ax, az, r + ay)
                    if ay:
                        total = total + pick(ax, az, r - ay)
                    for k, part in enumerate((ax, ay, az)):
                        if part:
                            weight = influence(square) * part**4 / math.sqrt(square) ** 3
                            energy[k] = energy[k] + weight * total
            alive = vol_ext[r, at : at + SUB, :] > 0
            for k in range(3):
                safe = jnp.where(alive, energy[k], 1.0)
                put(3 + k, y, at, jnp.where(alive, bulk / safe, 1.0))
        return carry

    lax.fori_loop(0, ext.shape[1], factor_row, 0)

    def factor_out(y, carry):
        for k in range(3):
            fac_out[k, y, :, :] = ext[(3 + k) * 5 + 2, y + HORIZON, left : left + cols, :]
        return carry

    lax.fori_loop(0, rows, factor_out, 0)

    for side, delta in enumerate(SIDES):
        arrived(disp_copy, (delta, 0))
    for side, at in ((0, left - HORIZON), (1, right)):

        def edge_row(y, carry):
            for k in range(3):
                value = got_x[side, pl.ds((k * rows + y) * HORIZON, HORIZON), :]
                put(k, y + HORIZON, at, position(k, value, y + HORIZON, at))
            return carry

        lax.fori_loop(0, rows, edge_row, 0)

    def halo_rows(side):
        delta = SIDES[side]
        for dx in (-1, 0, 1):
            arrived(disp_copy, (dx, delta))
        base = 0 if side == 0 else HORIZON + rows

        def halo_row(y, carry):
            row = y + base
            for k in range(3):
                for at in range(0, cols, SUB):
                    value = got_y[side, k, y, at : at + SUB, :]
                    put(k, row, left + at, position(k, value, row, left + at))
                for dx, at in ((-1, left - HORIZON), (1, right)):
                    corner = CORNERS.index((dx, delta))
                    value = got_c[corner, pl.ds((k * HORIZON + y) * HORIZON, HORIZON), :]
                    put(k, row, at, position(k, value, row, at))
            return carry

        lax.fori_loop(0, HORIZON, halo_row, 0)

    kinds = bond_types()

    def force_tile(y, tile):
        at = pl.multiple_of(tile * SUB, SUB)
        row = y + HORIZON

        def load(field, bond):
            ox, oy, oz = bond
            if abs(oz) <= 2:
                return ext[field * 5 + oz + 2, row + oy, pl.ds(at + (left + ox), SUB), :]
            value = shifted(own[field], oz)
            if field == 2:
                value = value + float(oz)
            if field == 6:
                inside = lane < LANES - oz if oz > 0 else lane >= -oz
                value = jnp.where(inside, value, 0.0)
            return value

        own = [ext[f * 5 + 2, row, pl.ds(at + left, SUB), :] for f in range(7)]
        force = [zero, zero, zero]
        for kind, bonds in kinds.items():
            square = sum(a * a for a in kind)
            length = math.sqrt(square)
            common = math.gcd(*kind)
            count = sum(a > 0 for a in kind)
            scale = 0.5 if count == 1 else length / (2.0 * common)
            scale = STIFF * influence(square) * scale
            total = [zero, zero, zero]
            for bond in bonds:
                apart = [load(k, bond) - own[k] for k in range(3)]
                squared = apart[0] * apart[0] + apart[1] * apart[1] + apart[2] * apart[2]
                pull = 1.0 / length - lax.rsqrt(squared)
                near = [k for k in range(3) if bond[k]]
                pair = {k: own[3 + k] + load(3 + k, bond) for k in near}
                if count == 1:
                    ratio = pair[near[0]]
                else:
                    two = {k: pair[k] * pair[k] for k in near}
                    part = {k: (bond[k] // common) ** 2 for k in near}
                    if count == 2:
                        a, b = near
                        left_term = two[b] if part[a] == 1 else two[b] * float(part[a])
                        right_term = two[a] if part[b] == 1 else two[a] * float(part[b])
                        ratio = pair[a] * pair[b] * lax.rsqrt(left_term + right_term)
                    else:
                        odd = next(
                            k for k in near if sum(part[j] == part[k] for j in near) in (1, 3)
                        )
                        a, b = [k for k in near if k != odd]
                        first = two[a] * two[b]
                        if part[odd] != 1:
                            first = first * float(part[odd])
                        second = two[odd] * (two[a] + two[b])
                        if part[a] != 1:
                            second = second * float(part[a])
                        ratio = pair[a] * pair[b] * pair[odd] * lax.rsqrt(first + second)
                factor = (ratio * pull) * load(6, bond)
                total = [total[k] + factor * apart[k] for k in range(3)]
            force = [force[k] + scale * total[k] for k in range(3)]
        alive = own[6] > 0
        for k in range(3):
            force_out[k, y, pl.ds(at, SUB), :] = jnp.where(alive, force[k], 0.0)

    def force_row(i, carry):
        y = lax.rem(i + HORIZON, rows)

        @pl.when(i == rows - 2 * HORIZON)
        def _():
            halo_rows(1)

        @pl.when(i == rows - HORIZON)
        def _():
            halo_rows(0)

        def one(tile, inner):
            force_tile(y, tile)
            return inner

        return lax.fori_loop(0, cols // SUB, one, carry)

    lax.fori_loop(0, rows, force_row, 0)

    for make in (vol_copy, disp_copy):
        for step in order:

            @pl.when(has(step))
            def _():
                make(step).wait_send()


def shards(displacement, volume, material, layers):
    _, rows, cols, depth = displacement.shape
    wide_rows, wide_cols = rows + 2 * WIDE, cols + 2 * SUB
    near_rows = rows + 2 * HORIZON
    near_tiles = -(-(cols + 2 * HORIZON) // SUB)
    vmem = pl.BlockSpec(memory_space=pltpu.VMEM)
    edge = -(-3 * rows * HORIZON // SUB) * SUB
    corner = -(-3 * HORIZON * HORIZON // SUB) * SUB
    result = jax.ShapeDtypeStruct((3, rows, cols, depth), jnp.float32)

    def scratch(*shape):
        return pltpu.VMEM(shape + (depth,), jnp.float32)

    return pl.pallas_call(
        kernel,
        out_shape=(result, result),
        in_specs=[vmem] * 4,
        out_specs=(vmem, vmem),
        scratch_shapes=[
            scratch(wide_rows, wide_cols),
            scratch(HORIZON, wide_rows, wide_cols),
            scratch(len(TPAIRS), wide_rows, near_tiles * SUB),
            scratch(35, near_rows, wide_cols),
            scratch(2, edge),
            scratch(4, corner),
            scratch(2, 3, HORIZON, cols),
            scratch(2, edge),
            scratch(4, corner),
            pltpu.SemaphoreType.DMA((4, len(STEPS))),
        ],
        compiler_params=pltpu.CompilerParams(collective_id=0, has_side_effects=True),
        name="bonds",
    )(displacement, volume, material, layers)


def solution(mesh):
    return jax.shard_map(
        shards,
        mesh=mesh,
        in_specs=(P(None, "gy", "gx", None), P("gy", "gx", None), P("gy", "gx"), P("gy", "gx")),
        out_specs=(P(None, "gy", "gx", None), P(None, "gy", "gx", None)),
        check_vma=False,
    )
```

```python
import math

import jax
import jax.numpy as jnp
from jax import lax
from jax.experimental import pallas as pl
from jax.experimental.pallas import tpu as pltpu
from jax.sharding import PartitionSpec as P

HORIZON = 3
STIFF = 5.0
WIDE = 2 * HORIZON
LANES = 128
SUB = 8
MESH = pl.DeviceIdType.MESH
SIDES = (-1, 1)
STEPS = tuple((dx, dy) for dy in (-1, 0, 1) for dx in (-1, 0, 1) if (dx, dy) != (0, 0))
CORNERS = tuple(step for step in STEPS if step[0] and step[1])


def bond_list():
    reach = range(-HORIZON, HORIZON + 1)
    return [
        (x, y, z)
        for y in reach
        for x in reach
        for z in reach
        if 0 < x * x + y * y + z * z <= HORIZON * HORIZON
    ]


def bond_types(oz):
    kinds = {}
    for bond in bond_list():
        if bond[2] == oz:
            kinds.setdefault(tuple(sorted(map(abs, bond))), []).append(bond)
    return kinds


def influence(square):
    return (1.0 - square / (HORIZON * HORIZON)) ** 2


def moved(value, step):
    return pltpu.roll(value, (-step) % LANES, 1) if step else value


def kernel(
    disp_in, volume_in, material_in, layers_in, fac_out, force_out,
    disp, volume, material, layers, vol_ext, ext, force_buf,
    send_xv, send_cv, send_x, send_c, got_xv, got_cv, got_y, got_x, got_c,
    sems, load_sems, out_sems, fac_sem,
):
    rows, cols = volume.shape[0], volume.shape[1]
    left = SUB
    right = left + cols
    bottom = WIDE + rows
    gx, gy = lax.axis_index("gx"), lax.axis_index("gy")
    nx, ny = lax.axis_size("gx"), lax.axis_size("gy")

    def has(step):
        dx, dy = step
        found = None
        for delta, at, size in ((dx, gx, nx), (dy, gy, ny)):
            if delta:
                test = at > 0 if delta < 0 else at < size - 1
                found = test if found is None else found & test
        return found

    def device(step):
        return {"gx": gx + step[0], "gy": gy + step[1]}

    barrier = pltpu.get_barrier_semaphore()
    for step in STEPS:

        @pl.when(has(step))
        def _():
            pl.semaphore_signal(barrier, inc=1, device_id=device(step), device_id_type=MESH)

    loads = [
        pltpu.make_async_copy(source, target, load_sems.at[index])
        for index, (source, target) in enumerate(
            ((material_in, material), (layers_in, layers), (volume_in, volume), (disp_in, disp))
        )
    ]
    for copy in loads:
        copy.start()

    lane = lax.broadcasted_iota(jnp.int32, (SUB, LANES), 1)
    sub_f = lax.broadcasted_iota(jnp.int32, (SUB, LANES), 0).astype(jnp.float32)
    zero = jnp.zeros((SUB, LANES), jnp.float32)

    def clear(ref, *where):
        ref[where] = jnp.zeros(ref.at[where].shape, jnp.float32)

    @pl.when(gy == 0)
    def _():
        clear(vol_ext, slice(0, WIDE), slice(left, right))
        clear(got_y, 0)

    @pl.when(gy == ny - 1)
    def _():
        clear(vol_ext, slice(bottom, bottom + WIDE), slice(left, right))
        clear(got_y, 1)

    for side, delta in enumerate(SIDES):

        @pl.when(jnp.logical_not(has((delta, 0))))
        def _():
            clear(got_xv, side)
            clear(got_x, side)

    for index, step in enumerate(CORNERS):

        @pl.when(jnp.logical_not(has(step)))
        def _():
            clear(got_cv, index)
            clear(got_c, index)

    for copy in loads[:3]:
        copy.wait()
    eye_row = lax.broadcasted_iota(jnp.int32, (cols, cols), 0)
    eye_col = lax.broadcasted_iota(jnp.int32, (cols, cols), 1)
    level = lax.broadcasted_iota(jnp.int32, (cols, LANES), 1).astype(jnp.float32)
    filled = jnp.where(material[...] > 0, layers[...], 0).astype(jnp.float32)
    for y in range(rows):
        line = jnp.broadcast_to(filled[y : y + 1, :], (cols, cols))
        top = jnp.sum(jnp.where(eye_row == eye_col, line, 0.0), axis=1, keepdims=True)
        vol_ext[WIDE + y, left:right, :] = jnp.where(
            level < jnp.broadcast_to(top, (cols, LANES)), volume[y], 0.0
        )

    loads[3].wait()
    for side, delta in enumerate(SIDES):
        first = left if delta < 0 else right - WIDE
        for y in range(rows):
            send_xv[side, y * WIDE : (y + 1) * WIDE, :] = vol_ext[WIDE + y, first : first + WIDE, :]
        first = 0 if delta < 0 else cols - HORIZON
        for k in range(3):
            for y in range(rows):
                at = (k * rows + y) * HORIZON
                send_x[side, at : at + HORIZON, :] = disp[k, y, first : first + HORIZON, :]
    for index, (dx, dy) in enumerate(CORNERS):
        first = left if dx < 0 else right - WIDE
        start = WIDE if dy < 0 else bottom - WIDE
        for y in range(WIDE):
            at = y * WIDE
            send_cv[index, at : at + WIDE, :] = vol_ext[start + y, first : first + WIDE, :]
        first = 0 if dx < 0 else cols - HORIZON
        start = 0 if dy < 0 else rows - HORIZON
        for k in range(3):
            for y in range(HORIZON):
                at = (k * HORIZON + y) * HORIZON
                send_c[index, at : at + HORIZON, :] = disp[k, start + y, first : first + HORIZON, :]

    middle_x = left + cols // 2
    middle_y = HORIZON + rows // 2

    def place(k, value, y, at):
        width = value.shape[0]
        if k == 0:
            value = value + (sub_f[:width] + float(at - middle_x))
        if k == 1:
            value = value + (y - middle_y).astype(jnp.float32)
        ext[k, y, at : at + width, :] = value

    def own_row(y, carry):
        for k in range(3):
            for at in range(0, cols, SUB):
                place(k, disp[k, y, at : at + SUB, :], y + HORIZON, left + at)
        return carry

    lax.fori_loop(0, rows, own_row, 0)

    peers = sum(has(step).astype(jnp.int32) for step in STEPS)
    pl.semaphore_wait(barrier, peers)

    def cut_from(delta, size, width):
        return {-1: (0, width), 0: (0, size), 1: (size - width, width)}[delta]

    def vol_copy(step):
        dx, dy = step
        if dx == 0:
            y0 = WIDE if dy < 0 else bottom - WIDE
            to_y = bottom if dy < 0 else 0
            source = vol_ext.at[y0 : y0 + WIDE, left:right]
            target = vol_ext.at[to_y : to_y + WIDE, left:right]
        elif dy == 0:
            source, target = send_xv.at[0 if dx < 0 else 1], got_xv.at[0 if dx > 0 else 1]
        else:
            source, target = send_cv.at[CORNERS.index(step)], got_cv.at[CORNERS.index((-dx, -dy))]
        return pltpu.make_async_remote_copy(
            src_ref=source,
            dst_ref=target,
            send_sem=sems.at[0, STEPS.index(step)],
            recv_sem=sems.at[1, STEPS.index((-dx, -dy))],
            device_id=device(step),
            device_id_type=MESH,
        )

    def disp_copy(step):
        dx, dy = step
        if dx == 0:
            y0, yn = cut_from(dy, rows, HORIZON)
            source, target = disp.at[:, y0 : y0 + yn], got_y.at[0 if dy > 0 else 1]
        elif dy == 0:
            source, target = send_x.at[0 if dx < 0 else 1], got_x.at[0 if dx > 0 else 1]
        else:
            source, target = send_c.at[CORNERS.index(step)], got_c.at[CORNERS.index((-dx, -dy))]
        return pltpu.make_async_remote_copy(
            src_ref=source,
            dst_ref=target,
            send_sem=sems.at[2, STEPS.index(step)],
            recv_sem=sems.at[3, STEPS.index((-dx, -dy))],
            device_id=device(step),
            device_id_type=MESH,
        )

    order = sorted(STEPS, key=lambda step: (-abs(step[0]) - abs(step[1]), -abs(step[0])))
    for make in (vol_copy, disp_copy):
        for step in order:

            @pl.when(has(step))
            def _():
                make(step).start()

    def arrived(make, step):
        @pl.when(has(step))
        def _():
            dx, dy = step
            make((-dx, -dy)).wait_recv()

    for step in order:
        arrived(vol_copy, step)
    for side in range(2):
        first = left - WIDE if side == 0 else right
        for y in range(rows):
            at = y * WIDE
            vol_ext[WIDE + y, first : first + WIDE, :] = got_xv[side, at : at + WIDE, :]
    for index, (dx, dy) in enumerate(CORNERS):
        first = left - WIDE if dx < 0 else right
        start = 0 if dy < 0 else bottom
        for y in range(WIDE):
            at = y * WIDE
            vol_ext[start + y, first : first + WIDE, :] = got_cv[index, at : at + WIDE, :]

    bulk = math.pi * HORIZON**4 / 30.0
    near_rows = ext.shape[1]
    near_tiles = -(-(cols + 2 * HORIZON) // SUB)

    def inside(step):
        return lane < LANES - step if step > 0 else lane >= -step

    def factor_tile(y, at):
        row = y + HORIZON
        beside = {}
        for ax in range(HORIZON + 1):
            for ay in range(HORIZON + 1):
                if ax * ax + ay * ay > HORIZON * HORIZON:
                    continue
                total = None
                for dy in sorted({ay, -ay}):
                    for dx in sorted({ax, -ax}):
                        term = vol_ext[row + dy, at + dx : at + dx + SUB, :]
                        total = term if total is None else total + term
                beside[ax, ay] = total
        energy = [None, None, None]
        for k in range(3):
            for az in range(HORIZON + 1):
                layer = None
                for (ax, ay), total in beside.items():
                    square = ax * ax + ay * ay + az * az
                    part = (ax, ay, az)[k]
                    if not 0 < square <= HORIZON * HORIZON or not part:
                        continue
                    term = (influence(square) * part**4 / math.sqrt(square) ** 3) * total
                    layer = term if layer is None else layer + term
                if layer is None:
                    continue
                if az:
                    ahead = jnp.where(inside(az), moved(layer, az), 0.0)
                    layer = ahead + jnp.where(inside(-az), moved(layer, -az), 0.0)
                energy[k] = layer if energy[k] is None else energy[k] + layer
        alive = vol_ext[row, at : at + SUB, :] > 0
        for k in range(3):
            safe = jnp.where(alive, energy[k], 1.0)
            ext[3 + k, y, at : at + SUB, :] = jnp.where(alive, bulk / safe, 1.0)

    def factor_rows(i, carry):
        for y in range(2):
            for tile in range(near_tiles):
                factor_tile(i * 2 + y, left - HORIZON + tile * SUB)
        return carry

    lax.fori_loop(0, near_rows // 2, factor_rows, 0)
    own_rows = slice(HORIZON, HORIZON + rows)
    fac_copy = pltpu.make_async_copy(ext.at[3:6, own_rows, left:right], fac_out, fac_sem)
    fac_copy.start()

    for side, delta in enumerate(SIDES):
        arrived(disp_copy, (delta, 0))
    for side, at in ((0, left - HORIZON), (1, right)):

        def edge_row(y, carry):
            for k in range(3):
                value = got_x[side, pl.ds((k * rows + y) * HORIZON, HORIZON), :]
                place(k, value, y + HORIZON, at)
            return carry

        lax.fori_loop(0, rows, edge_row, 0)

    def halo_rows(side):
        delta = SIDES[side]
        for dx in (-1, 0, 1):
            arrived(disp_copy, (dx, delta))
        base = 0 if side == 0 else HORIZON + rows

        def halo_row(y, carry):
            row = y + base
            for k in range(3):
                for at in range(0, cols, SUB):
                    place(k, got_y[side, k, y, at : at + SUB, :], row, left + at)
                for dx, at in ((-1, left - HORIZON), (1, right)):
                    corner = CORNERS.index((dx, delta))
                    value = got_c[corner, pl.ds((k * HORIZON + y) * HORIZON, HORIZON), :]
                    place(k, value, row, at)
            return carry

        lax.fori_loop(0, HORIZON, halo_row, 0)

    def force_tile(y, tile):
        start = pl.multiple_of(tile * SUB, SUB)
        row = y + HORIZON

        def load(field, ox, oy):
            at = pl.ds(start + (left + ox), SUB)
            if field == 6:
                return vol_ext[row + HORIZON + oy, at, :]
            return ext[field, row + oy, at, :]

        own = [load(f, 0, 0) for f in range(6)]
        force = [None, None, None]
        for oz in sorted(range(-HORIZON, HORIZON + 1), key=abs):
            kinds = bond_types(oz)
            mine = [moved(value, -oz) for value in own]
            if oz:
                mine[2] = mine[2] - float(oz)
            summed = [None, None, None]

            def add(sums, factor, values):
                for k in range(3):
                    term = factor * values[k]
                    sums[k] = term if sums[k] is None else sums[k] + term

            for kind, bonds in kinds.items():
                square = sum(a * a for a in kind)
                length = math.sqrt(square)
                common = math.gcd(*kind)
                count = sum(a > 0 for a in kind)
                scale = 0.5 if count == 1 else length / (2.0 * common)
                scale = STIFF * influence(square) * scale
                late = len(bonds) > 6
                total = [None, None, None]
                for bond in bonds:
                    ox, oy, _ = bond
                    apart = [load(k, ox, oy) - mine[k] for k in range(3)]
                    squared = apart[0] * apart[0] + apart[1] * apart[1] + apart[2] * apart[2]
                    if late:
                        pull = 1.0 / length - lax.rsqrt(squared)
                    else:
                        pull = scale / length - scale * lax.rsqrt(squared)
                    near = [k for k in range(3) if bond[k]]
                    pair = {k: mine[3 + k] + load(3 + k, ox, oy) for k in near}
                    if count == 1:
                        ratio = pair[near[0]]
                    else:
                        two = {k: pair[k] * pair[k] for k in near}
                        part = {k: (bond[k] // common) ** 2 for k in near}
                        if count == 2:
                            a, b = near
                            first = two[b] if part[a] == 1 else two[b] * float(part[a])
                            second = two[a] if part[b] == 1 else two[a] * float(part[b])
                            ratio = pair[a] * pair[b] * lax.rsqrt(first + second)
                        else:
                            odd = next(
                                k for k in near if sum(part[j] == part[k] for j in near) in (1, 3)
                            )
                            a, b = [k for k in near if k != odd]
                            first = two[a] * two[b]
                            if part[odd] != 1:
                                first = first * float(part[odd])
                            second = two[odd] * (two[a] + two[b])
                            if part[a] != 1:
                                second = second * float(part[a])
                            ratio = pair[a] * pair[b] * pair[odd] * lax.rsqrt(first + second)
                    factor = (ratio * pull) * load(6, ox, oy)
                    add(total if late else summed, factor, apart)
                if late:
                    add(summed, scale, total)
            if oz:
                summed = [jnp.where(inside(oz), moved(value, oz), 0.0) for value in summed]
                force = [force[k] + summed[k] for k in range(3)]
            else:
                force = summed
        alive = load(6, 0, 0) > 0
        for k in range(3):
            force_buf[k, y, pl.ds(start, SUB), :] = jnp.where(alive, force[k], 0.0)

    def out_copy(y):
        return pltpu.make_async_copy(force_buf.at[:, y], force_out.at[:, y], out_sems.at[y])

    def force_row(i, carry):
        y = lax.rem(i + HORIZON, rows)

        @pl.when(i == rows - 2 * HORIZON)
        def _():
            halo_rows(1)

        @pl.when(i == rows - HORIZON)
        def _():
            halo_rows(0)

        def one(tile, inner):
            force_tile(y, tile)
            return inner

        lax.fori_loop(0, cols // SUB, one, 0)
        out_copy(y).start()
        return carry

    lax.fori_loop(0, rows, force_row, 0)

    for make in (vol_copy, disp_copy):
        for step in order:

            @pl.when(has(step))
            def _():
                make(step).wait_send()

    fac_copy.wait()
    for y in range(rows):
        out_copy(y).wait()


def shards(displacement, volume, material, layers):
    _, rows, cols, depth = displacement.shape
    wide_rows, wide_cols = rows + 2 * WIDE, cols + 2 * SUB
    near_rows = rows + 2 * HORIZON
    hbm = pl.BlockSpec(memory_space=pltpu.MemorySpace.HBM)
    result = jax.ShapeDtypeStruct((3, rows, cols, depth), jnp.float32)

    def whole(count):
        return -(-count // SUB) * SUB

    edge, corner = whole(3 * rows * HORIZON), whole(3 * HORIZON * HORIZON)
    edge_vol, corner_vol = whole(rows * WIDE), whole(WIDE * WIDE)

    def scratch(*shape):
        return pltpu.VMEM(shape + (depth,), jnp.float32)

    return pl.pallas_call(
        kernel,
        out_shape=(result, result),
        in_specs=[hbm] * 4,
        out_specs=(hbm, hbm),
        scratch_shapes=[
            scratch(3, rows, cols),
            scratch(rows, cols),
            pltpu.VMEM((rows, cols), jnp.int32),
            pltpu.VMEM((rows, cols), jnp.int32),
            scratch(wide_rows, wide_cols),
            scratch(6, near_rows, wide_cols),
            scratch(3, rows, cols),
            scratch(2, edge_vol),
            scratch(4, corner_vol),
            scratch(2, edge),
            scratch(4, corner),
            scratch(2, edge_vol),
            scratch(4, corner_vol),
            scratch(2, 3, HORIZON, cols),
            scratch(2, edge),
            scratch(4, corner),
            pltpu.SemaphoreType.DMA((4, len(STEPS))),
            pltpu.SemaphoreType.DMA((4,)),
            pltpu.SemaphoreType.DMA((rows,)),
            pltpu.SemaphoreType.DMA,
        ],
        compiler_params=pltpu.CompilerParams(collective_id=0, has_side_effects=True),
        name="bonds",
    )(displacement, volume, material, layers)


def solution(mesh):
    return jax.shard_map(
        shards,
        mesh=mesh,
        in_specs=(P(None, "gy", "gx", None), P("gy", "gx", None), P("gy", "gx"), P("gy", "gx")),
        out_specs=(P(None, "gy", "gx", None), P(None, "gy", "gx", None)),
        check_vma=False,
    )
```

```python
import math

import jax
import jax.numpy as jnp
from jax import lax
from jax.experimental import pallas as pl
from jax.experimental.pallas import tpu as pltpu
from jax.sharding import PartitionSpec as P

HORIZON = 3
STIFF = 5.0
WIDE = 2 * HORIZON
LANES = 128
VMEM_LIMIT = 24 * 2**20
SUB = 8
MESH = pl.DeviceIdType.MESH
SIDES = (-1, 1)
STEPS = tuple((dx, dy) for dy in (-1, 0, 1) for dx in (-1, 0, 1) if (dx, dy) != (0, 0))
CORNERS = tuple(step for step in STEPS if step[0] and step[1])


def bond_list():
    reach = range(-HORIZON, HORIZON + 1)
    return [
        (x, y, z)
        for y in reach
        for x in reach
        for z in reach
        if 0 < x * x + y * y + z * z <= HORIZON * HORIZON
    ]


def bond_types(oz):
    kinds = {}
    for bond in bond_list():
        if bond[2] == oz:
            kinds.setdefault(tuple(sorted(map(abs, bond))), []).append(bond)
    return kinds


def influence(square):
    return (1.0 - square / (HORIZON * HORIZON)) ** 2


AWAY = tuple(oz for oz in range(-HORIZON, HORIZON + 1) if oz)


def moved(value, step):
    return pltpu.roll(value, (-step) % LANES, 1) if step else value


def inside(lane, step):
    return lane < LANES - step if step > 0 else lane >= -step


def middle_row(rows, index):
    return lax.rem(index + HORIZON, rows)


def force_tile(vol_ext, ext, mine, sums, y, slot, tile):
    start = pl.multiple_of(tile * SUB, SUB)
    row = y + HORIZON

    def load(field, ox, oy):
        at = pl.ds(start + (SUB + ox), SUB)
        if field == 6:
            return vol_ext[row + HORIZON + oy, at, :]
        return ext[field, row + oy, at, :]

    for oz in sorted(range(-HORIZON, HORIZON + 1), key=abs):
        kinds = bond_types(oz)
        own = {}
        for f in range(6):
            if oz == 0:
                own[f] = load(f, 0, 0)
            elif f < 3 or f == 5 or abs(oz) < HORIZON:
                own[f] = mine[f, AWAY.index(oz), y, pl.ds(start + SUB, SUB), :]
        summed = [None, None, None]

        def add(sums, factor, values):
            for k in range(3):
                term = factor * values[k]
                sums[k] = term if sums[k] is None else sums[k] + term

        for kind, bonds in kinds.items():
            square = sum(a * a for a in kind)
            length = math.sqrt(square)
            common = math.gcd(*kind)
            count = sum(a > 0 for a in kind)
            scale = 0.5 if count == 1 else length / (2.0 * common)
            scale = STIFF * influence(square) * scale
            late = len(bonds) > 6
            total = [None, None, None]
            for bond in bonds:
                ox, oy, _ = bond
                apart = [load(k, ox, oy) - own[k] for k in range(3)]
                squared = apart[0] * apart[0] + apart[1] * apart[1] + apart[2] * apart[2]
                if late:
                    pull = 1.0 / length - lax.rsqrt(squared)
                else:
                    pull = scale / length - scale * lax.rsqrt(squared)
                near = [k for k in range(3) if bond[k]]
                pair = {k: own[3 + k] + load(3 + k, ox, oy) for k in near}
                if count == 1:
                    ratio = pair[near[0]]
                else:
                    two = {k: pair[k] * pair[k] for k in near}
                    part = {k: (bond[k] // common) ** 2 for k in near}
                    if count == 2:
                        a, b = near
                        first = two[b] if part[a] == 1 else two[b] * float(part[a])
                        second = two[a] if part[b] == 1 else two[a] * float(part[b])
                        ratio = pair[a] * pair[b] * lax.rsqrt(first + second)
                    else:
                        odd = next(
                            k for k in near if sum(part[j] == part[k] for j in near) in (1, 3)
                        )
                        a, b = [k for k in near if k != odd]
                        first = two[a] * two[b]
                        if part[odd] != 1:
                            first = first * float(part[odd])
                        second = two[odd] * (two[a] + two[b])
                        if part[a] != 1:
                            second = second * float(part[a])
                        ratio = pair[a] * pair[b] * pair[odd] * lax.rsqrt(first + second)
                factor = (ratio * pull) * load(6, ox, oy)
                add(total if late else summed, factor, apart)
            if late:
                add(summed, scale, total)
        for k in range(3):
            sums[k, oz + HORIZON, slot, pl.ds(start, SUB), :] = summed[k]


def kernel(
    disp_in, volume_in, material_in, layers_in, vol_ext, ext, mine, sums,
    disp, volume, material, layers,
    send_xv, send_cv, send_x, send_c, got_xv, got_cv, got_y, got_x, got_c,
    sems, load_sems,
):
    rows, cols = volume.shape[0], volume.shape[1]
    left = SUB
    right = left + cols
    bottom = WIDE + rows
    gx, gy = lax.axis_index("gx"), lax.axis_index("gy")
    nx, ny = lax.axis_size("gx"), lax.axis_size("gy")

    def has(step):
        dx, dy = step
        found = None
        for delta, at, size in ((dx, gx, nx), (dy, gy, ny)):
            if delta:
                test = at > 0 if delta < 0 else at < size - 1
                found = test if found is None else found & test
        return found

    def device(step):
        return {"gx": gx + step[0], "gy": gy + step[1]}

    barrier = pltpu.get_barrier_semaphore()
    for step in STEPS:

        @pl.when(has(step))
        def _():
            pl.semaphore_signal(barrier, inc=1, device_id=device(step), device_id_type=MESH)

    loads = [
        pltpu.make_async_copy(source, target, load_sems.at[index])
        for index, (source, target) in enumerate(
            ((material_in, material), (layers_in, layers), (volume_in, volume), (disp_in, disp))
        )
    ]
    for copy in loads:
        copy.start()

    lane = lax.broadcasted_iota(jnp.int32, (SUB, LANES), 1)
    sub_f = lax.broadcasted_iota(jnp.int32, (SUB, LANES), 0).astype(jnp.float32)
    zero = jnp.zeros((SUB, LANES), jnp.float32)

    def clear(ref, *where):
        ref[where] = jnp.zeros(ref.at[where].shape, jnp.float32)

    @pl.when(gy == 0)
    def _():
        clear(vol_ext, slice(0, WIDE), slice(left, right))
        clear(got_y, 0)

    @pl.when(gy == ny - 1)
    def _():
        clear(vol_ext, slice(bottom, bottom + WIDE), slice(left, right))
        clear(got_y, 1)

    for side, delta in enumerate(SIDES):

        @pl.when(jnp.logical_not(has((delta, 0))))
        def _():
            clear(got_xv, side)
            clear(got_x, side)

    for index, step in enumerate(CORNERS):

        @pl.when(jnp.logical_not(has(step)))
        def _():
            clear(got_cv, index)
            clear(got_c, index)

    for copy in loads[:3]:
        copy.wait()
    eye_row = lax.broadcasted_iota(jnp.int32, (cols, cols), 0)
    eye_col = lax.broadcasted_iota(jnp.int32, (cols, cols), 1)
    level = lax.broadcasted_iota(jnp.int32, (cols, LANES), 1).astype(jnp.float32)
    filled = jnp.where(material[...] > 0, layers[...], 0).astype(jnp.float32)
    for y in range(rows):
        line = jnp.broadcast_to(filled[y : y + 1, :], (cols, cols))
        top = jnp.sum(jnp.where(eye_row == eye_col, line, 0.0), axis=1, keepdims=True)
        vol_ext[WIDE + y, left:right, :] = jnp.where(
            level < jnp.broadcast_to(top, (cols, LANES)), volume[y], 0.0
        )

    loads[3].wait()
    for side, delta in enumerate(SIDES):
        first = left if delta < 0 else right - WIDE
        for y in range(rows):
            send_xv[side, y * WIDE : (y + 1) * WIDE, :] = vol_ext[WIDE + y, first : first + WIDE, :]
        first = 0 if delta < 0 else cols - HORIZON
        for k in range(3):
            for y in range(rows):
                at = (k * rows + y) * HORIZON
                send_x[side, at : at + HORIZON, :] = disp[k, y, first : first + HORIZON, :]
    for index, (dx, dy) in enumerate(CORNERS):
        first = left if dx < 0 else right - WIDE
        start = WIDE if dy < 0 else bottom - WIDE
        for y in range(WIDE):
            at = y * WIDE
            send_cv[index, at : at + WIDE, :] = vol_ext[start + y, first : first + WIDE, :]
        first = 0 if dx < 0 else cols - HORIZON
        start = 0 if dy < 0 else rows - HORIZON
        for k in range(3):
            for y in range(HORIZON):
                at = (k * HORIZON + y) * HORIZON
                send_c[index, at : at + HORIZON, :] = disp[k, start + y, first : first + HORIZON, :]

    middle_x = left + cols // 2
    middle_y = HORIZON + rows // 2

    def place(k, value, y, at):
        width = value.shape[0]
        if k == 0:
            value = value + (sub_f[:width] + float(at - middle_x))
        if k == 1:
            value = value + (y - middle_y).astype(jnp.float32)
        ext[k, y, at : at + width, :] = value

    def own_row(y, carry):
        for at in range(0, cols, SUB):
            for k in range(3):
                place(k, disp[k, y, at : at + SUB, :], y + HORIZON, left + at)
                value = ext[k, y + HORIZON, left + at : left + at + SUB, :]
                for oz in AWAY:
                    there = moved(value, -oz)
                    if k == 2:
                        there = there - float(oz)
                    mine[k, AWAY.index(oz), y, left + at : left + at + SUB, :] = there
        return carry

    lax.fori_loop(0, rows, own_row, 0)

    peers = sum(has(step).astype(jnp.int32) for step in STEPS)
    pl.semaphore_wait(barrier, peers)

    def cut_from(delta, size, width):
        return {-1: (0, width), 0: (0, size), 1: (size - width, width)}[delta]

    def vol_copy(step):
        dx, dy = step
        if dx == 0:
            y0 = WIDE if dy < 0 else bottom - WIDE
            to_y = bottom if dy < 0 else 0
            source = vol_ext.at[y0 : y0 + WIDE, left:right]
            target = vol_ext.at[to_y : to_y + WIDE, left:right]
        elif dy == 0:
            source, target = send_xv.at[0 if dx < 0 else 1], got_xv.at[0 if dx > 0 else 1]
        else:
            source, target = send_cv.at[CORNERS.index(step)], got_cv.at[CORNERS.index((-dx, -dy))]
        return pltpu.make_async_remote_copy(
            src_ref=source,
            dst_ref=target,
            send_sem=sems.at[0, STEPS.index(step)],
            recv_sem=sems.at[1, STEPS.index((-dx, -dy))],
            device_id=device(step),
            device_id_type=MESH,
        )

    def disp_copy(step):
        dx, dy = step
        if dx == 0:
            y0, yn = cut_from(dy, rows, HORIZON)
            source, target = disp.at[:, y0 : y0 + yn], got_y.at[0 if dy > 0 else 1]
        elif dy == 0:
            source, target = send_x.at[0 if dx < 0 else 1], got_x.at[0 if dx > 0 else 1]
        else:
            source, target = send_c.at[CORNERS.index(step)], got_c.at[CORNERS.index((-dx, -dy))]
        return pltpu.make_async_remote_copy(
            src_ref=source,
            dst_ref=target,
            send_sem=sems.at[2, STEPS.index(step)],
            recv_sem=sems.at[3, STEPS.index((-dx, -dy))],
            device_id=device(step),
            device_id_type=MESH,
        )

    order = sorted(STEPS, key=lambda step: (-abs(step[0]) - abs(step[1]), -abs(step[0])))
    for make in (vol_copy, disp_copy):
        for step in order:

            @pl.when(has(step))
            def _():
                make(step).start()

    def arrived(make, step):
        @pl.when(has(step))
        def _():
            dx, dy = step
            make((-dx, -dy)).wait_recv()

    for step in order:
        arrived(vol_copy, step)
    for side in range(2):
        first = left - WIDE if side == 0 else right
        for y in range(rows):
            at = y * WIDE
            vol_ext[WIDE + y, first : first + WIDE, :] = got_xv[side, at : at + WIDE, :]
    for index, (dx, dy) in enumerate(CORNERS):
        first = left - WIDE if dx < 0 else right
        start = 0 if dy < 0 else bottom
        for y in range(WIDE):
            at = y * WIDE
            vol_ext[start + y, first : first + WIDE, :] = got_cv[index, at : at + WIDE, :]

    bulk = math.pi * HORIZON**4 / 30.0
    near_rows = ext.shape[1]
    near_tiles = -(-(cols + 2 * HORIZON) // SUB)

    def factor_tile(y, at):
        row = y + HORIZON
        beside = {}
        for ax in range(HORIZON + 1):
            for ay in range(HORIZON + 1):
                if ax * ax + ay * ay > HORIZON * HORIZON:
                    continue
                total = None
                for dy in sorted({ay, -ay}):
                    for dx in sorted({ax, -ax}):
                        term = vol_ext[row + dy, at + dx : at + dx + SUB, :]
                        total = term if total is None else total + term
                beside[ax, ay] = total
        energy = [None, None, None]
        for k in range(3):
            for az in range(HORIZON + 1):
                layer = None
                for (ax, ay), total in beside.items():
                    square = ax * ax + ay * ay + az * az
                    part = (ax, ay, az)[k]
                    if not 0 < square <= HORIZON * HORIZON or not part:
                        continue
                    term = (influence(square) * part**4 / math.sqrt(square) ** 3) * total
                    layer = term if layer is None else layer + term
                if layer is None:
                    continue
                if az:
                    ahead = jnp.where(inside(lane, az), moved(layer, az), 0.0)
                    layer = ahead + jnp.where(inside(lane, -az), moved(layer, -az), 0.0)
                energy[k] = layer if energy[k] is None else energy[k] + layer
        alive = vol_ext[row, at : at + SUB, :] > 0
        for k in range(3):
            safe = jnp.where(alive, energy[k], 1.0)
            ext[3 + k, y, at : at + SUB, :] = jnp.where(alive, bulk / safe, 1.0)

    def factor_rows(i, carry):
        for y in range(2):
            for tile in range(near_tiles):
                factor_tile(i * 2 + y, left - HORIZON + tile * SUB)
        return carry

    lax.fori_loop(0, near_rows // 2, factor_rows, 0)

    def factor_moved(i, carry):
        for part in range(4):
            y = i * 4 + part
            for at in range(left, right, SUB):
                for k in range(3):
                    value = ext[3 + k, y + HORIZON, at : at + SUB, :]
                    for oz in AWAY:
                        if k == 2 or abs(oz) < HORIZON:
                            mine[3 + k, AWAY.index(oz), y, at : at + SUB, :] = moved(value, -oz)
        return carry

    lax.fori_loop(0, rows // 4, factor_moved, 0)

    for side, delta in enumerate(SIDES):
        arrived(disp_copy, (delta, 0))
    for side, at in ((0, left - HORIZON), (1, right)):

        def edge_row(y, carry):
            for k in range(3):
                value = got_x[side, pl.ds((k * rows + y) * HORIZON, HORIZON), :]
                place(k, value, y + HORIZON, at)
            return carry

        lax.fori_loop(0, rows, edge_row, 0)

    def halo_rows(side):
        delta = SIDES[side]
        for dx in (-1, 0, 1):
            arrived(disp_copy, (dx, delta))
        base = 0 if side == 0 else HORIZON + rows

        def halo_row(y, carry):
            row = y + base
            for k in range(3):
                for at in range(0, cols, SUB):
                    place(k, got_y[side, k, y, at : at + SUB, :], row, left + at)
                for dx, at in ((-1, left - HORIZON), (1, right)):
                    corner = CORNERS.index((dx, delta))
                    value = got_c[corner, pl.ds((k * HORIZON + y) * HORIZON, HORIZON), :]
                    place(k, value, row, at)
            return carry

        lax.fori_loop(0, HORIZON, halo_row, 0)

    def row(i, carry):
        def one(tile, inner):
            force_tile(vol_ext, ext, mine, sums, middle_row(rows, i), i, tile)
            return inner

        return lax.fori_loop(0, cols // SUB, one, carry)

    lax.fori_loop(0, rows - 2 * HORIZON, row, 0)
    for side in (1, 0):
        halo_rows(side)

    for make in (vol_copy, disp_copy):
        for step in order:

            @pl.when(has(step))
            def _():
                make(step).wait_send()


def rest(
    vol_ext, ext, mine, early, fac_out, force_out, sums, force, out_sems, fac_sem
):
    rows, cols = force.shape[1], force.shape[2]
    lane = lax.broadcasted_iota(jnp.int32, (SUB, LANES), 1)
    own = ext.at[3:6, HORIZON : HORIZON + rows, SUB : SUB + cols]
    fac_copy = pltpu.make_async_copy(own, fac_out, fac_sem)
    fac_copy.start()
    done = early.shape[2]
    half = sums.shape[2]

    def out_copy(y):
        return pltpu.make_async_copy(force.at[:, y], force_out.at[:, y], out_sems.at[y])

    def finish(parts, slot, y):
        for at in range(0, cols, SUB):
            alive = vol_ext[y + WIDE, SUB + at : 2 * SUB + at, :] > 0
            for k in range(3):
                total = parts[k, HORIZON, slot, at : at + SUB, :]
                for oz in AWAY:
                    part = moved(parts[k, oz + HORIZON, slot, at : at + SUB, :], oz)
                    total = total + jnp.where(inside(lane, oz), part, 0.0)
                force[k, y, at : at + SUB, :] = jnp.where(alive, total, 0.0)
        out_copy(y).start()

    def group(first, carry):
        def row(slot, inner):
            y = middle_row(rows, first * half + slot + done)

            def one(tile, last):
                force_tile(vol_ext, ext, mine, sums, y, slot, tile)
                return last

            return lax.fori_loop(0, cols // SUB, one, inner)

        lax.fori_loop(0, half, row, 0)
        for slot in range(half):
            finish(sums, slot, middle_row(rows, first * half + slot + done))
        return carry

    for slot in range(done):
        finish(early, slot, (slot + HORIZON) % rows)
    lax.fori_loop(0, (rows - done) // half, group, 0)
    fac_copy.wait()
    for y in range(rows):
        out_copy(y).wait()


def shards(displacement, volume, material, layers):
    _, rows, cols, depth = displacement.shape
    wide_rows, wide_cols = rows + 2 * WIDE, cols + 2 * SUB
    near_rows = rows + 2 * HORIZON
    hbm = pl.BlockSpec(memory_space=pltpu.MemorySpace.HBM)
    result = jax.ShapeDtypeStruct((3, rows, cols, depth), jnp.float32)

    def whole(count):
        return -(-count // SUB) * SUB

    edge, corner = whole(3 * rows * HORIZON), whole(3 * HORIZON * HORIZON)
    edge_vol, corner_vol = whole(rows * WIDE), whole(WIDE * WIDE)

    def scratch(*shape):
        return pltpu.VMEM(shape + (depth,), jnp.float32)

    def held(*shape):
        return pltpu.VMEM(shape + (depth,), jnp.float32)

    def pin(values, space):
        return [pltpu.with_memory_space_constraint(value, space) for value in values]

    vmem = pl.BlockSpec(memory_space=pltpu.VMEM)
    early = rows - 2 * HORIZON
    frames = 2 * HORIZON + 1
    state = pl.pallas_call(
        kernel,
        out_shape=(
            held(wide_rows, wide_cols),
            held(6, near_rows, wide_cols),
            held(6, len(AWAY), rows, wide_cols),
            held(3, frames, early, cols),
        ),
        in_specs=[hbm] * 4,
        out_specs=(vmem,) * 4,
        scratch_shapes=[
            scratch(3, rows, cols),
            scratch(rows, cols),
            pltpu.VMEM((rows, cols), jnp.int32),
            pltpu.VMEM((rows, cols), jnp.int32),
            scratch(2, edge_vol),
            scratch(4, corner_vol),
            scratch(2, edge),
            scratch(4, corner),
            scratch(2, edge_vol),
            scratch(4, corner_vol),
            scratch(2, 3, HORIZON, cols),
            scratch(2, edge),
            scratch(4, corner),
            pltpu.SemaphoreType.DMA((4, len(STEPS))),
            pltpu.SemaphoreType.DMA((4,)),
        ],
        compiler_params=pltpu.CompilerParams(
            collective_id=0, has_side_effects=True, vmem_limit_bytes=VMEM_LIMIT
        ),
        name="gather",
    )(*pin((displacement, volume, material, layers), pltpu.MemorySpace.HBM))
    return pl.pallas_call(
        rest,
        out_shape=(result, result),
        in_specs=[vmem] * 4,
        out_specs=(hbm, hbm),
        scratch_shapes=[
            scratch(3, frames, HORIZON, cols),
            scratch(3, rows, cols),
            pltpu.SemaphoreType.DMA((rows,)),
            pltpu.SemaphoreType.DMA,
        ],
        compiler_params=pltpu.CompilerParams(vmem_limit_bytes=VMEM_LIMIT),
        name="rest",
    )(*pin(state, pltpu.MemorySpace.VMEM))


def solution(mesh):
    return jax.shard_map(
        shards,
        mesh=mesh,
        in_specs=(P(None, "gy", "gx", None), P("gy", "gx", None), P("gy", "gx"), P("gy", "gx")),
        out_specs=(P(None, "gy", "gx", None), P(None, "gy", "gx", None)),
        check_vma=False,
    )
```

```python
import math

import jax
import jax.numpy as jnp
from jax import lax
from jax.experimental import pallas as pl
from jax.experimental.pallas import tpu as pltpu
from jax.sharding import PartitionSpec as P

HORIZON = 3
STIFF = 5.0
WIDE = 2 * HORIZON
LANES = 128
VMEM_LIMIT = 24 * 2**20
SUB = 8
MESH = pl.DeviceIdType.MESH
SIDES = (-1, 1)
STEPS = tuple((dx, dy) for dy in (-1, 0, 1) for dx in (-1, 0, 1) if (dx, dy) != (0, 0))
CORNERS = tuple(step for step in STEPS if step[0] and step[1])


def bond_list():
    reach = range(-HORIZON, HORIZON + 1)
    return [
        (x, y, z)
        for y in reach
        for x in reach
        for z in reach
        if 0 < x * x + y * y + z * z <= HORIZON * HORIZON
    ]


def bond_types(oz):
    kinds = {}
    for bond in bond_list():
        if bond[2] == oz:
            kinds.setdefault(tuple(sorted(map(abs, bond))), []).append(bond)
    return kinds


def influence(square):
    return (1.0 - square / (HORIZON * HORIZON)) ** 2


AWAY = tuple(oz for oz in range(-HORIZON, HORIZON + 1) if oz)


def moved(value, step):
    return pltpu.roll(value, (-step) % LANES, 1) if step else value


def inside(lane, step):
    return lane < LANES - step if step > 0 else lane >= -step


def middle_row(rows, index):
    return lax.rem(index + HORIZON, rows)


def force_tile(vol_ext, ext, mine, sums, y, slot, tile):
    start = pl.multiple_of(tile * SUB, SUB)
    row = y + HORIZON

    def load(field, ox, oy):
        at = pl.ds(start + (SUB + ox), SUB)
        if field == 6:
            return vol_ext[row + HORIZON + oy, at, :]
        return ext[field, row + oy, at, :]

    for oz in sorted(range(-HORIZON, HORIZON + 1), key=abs):
        kinds = bond_types(oz)
        own = {}
        for f in range(6):
            if oz == 0:
                own[f] = load(f, 0, 0)
            elif f < 3 or f == 5 or abs(oz) < HORIZON:
                own[f] = mine[f, AWAY.index(oz), y, pl.ds(start + SUB, SUB), :]
        summed = [None, None, None]

        def add(sums, factor, values):
            for k in range(3):
                term = factor * values[k]
                sums[k] = term if sums[k] is None else sums[k] + term

        for kind, bonds in kinds.items():
            square = sum(a * a for a in kind)
            length = math.sqrt(square)
            common = math.gcd(*kind)
            count = sum(a > 0 for a in kind)
            scale = 0.5 if count == 1 else length / (2.0 * common)
            scale = STIFF * influence(square) * scale
            late = len(bonds) > 6
            total = [None, None, None]
            for bond in bonds:
                ox, oy, _ = bond
                apart = [load(k, ox, oy) - own[k] for k in range(3)]
                squared = apart[0] * apart[0] + apart[1] * apart[1] + apart[2] * apart[2]
                if late:
                    pull = 1.0 / length - lax.rsqrt(squared)
                else:
                    pull = scale / length - scale * lax.rsqrt(squared)
                near = [k for k in range(3) if bond[k]]
                pair = {k: own[3 + k] + load(3 + k, ox, oy) for k in near}
                if count == 1:
                    ratio = pair[near[0]]
                else:
                    two = {k: pair[k] * pair[k] for k in near}
                    part = {k: (bond[k] // common) ** 2 for k in near}
                    if count == 2:
                        a, b = near
                        first = two[b] if part[a] == 1 else two[b] * float(part[a])
                        second = two[a] if part[b] == 1 else two[a] * float(part[b])
                        ratio = pair[a] * pair[b] * lax.rsqrt(first + second)
                    else:
                        odd = next(
                            k for k in near if sum(part[j] == part[k] for j in near) in (1, 3)
                        )
                        a, b = [k for k in near if k != odd]
                        first = two[a] * two[b]
                        if part[odd] != 1:
                            first = first * float(part[odd])
                        second = two[odd] * (two[a] + two[b])
                        if part[a] != 1:
                            second = second * float(part[a])
                        ratio = pair[a] * pair[b] * pair[odd] * lax.rsqrt(first + second)
                factor = (ratio * pull) * load(6, ox, oy)
                add(total if late else summed, factor, apart)
            if late:
                add(summed, scale, total)
        for k in range(3):
            sums[k, oz + HORIZON, slot, pl.ds(start, SUB), :] = summed[k]


def kernel(
    disp_in, volume_in, material_in, layers_in, vol_ext, ext, mine, sums,
    disp, volume, material, layers,
    send_xv, send_cn, send_cf, send_x, send_c, got_xv, got_cn, got_cf, got_y, got_x, got_c,
    via_xv, via_x, sems, via_sems, load_sems,
):
    rows, cols = volume.shape[0], volume.shape[1]
    left = SUB
    right = left + cols
    bottom = WIDE + rows
    gx, gy = lax.axis_index("gx"), lax.axis_index("gy")
    nx, ny = lax.axis_size("gx"), lax.axis_size("gy")

    def has(step):
        dx, dy = step
        found = None
        for delta, at, size in ((dx, gx, nx), (dy, gy, ny)):
            if delta:
                test = at > 0 if delta < 0 else at < size - 1
                found = test if found is None else found & test
        return found

    odd = lax.rem(gy, 2)
    toward = 1 - 2 * odd
    paired = (gy + toward >= 0) & (gy + toward < ny)

    def to_partner(dy):
        return odd == (1 if dy < 0 else 0)

    def direct(step):
        if step in CORNERS:
            return has(step) & jnp.logical_not(to_partner(step[1]))
        return has(step)

    def device(step):
        return {"gx": gx + step[0], "gy": gy + step[1]}

    barrier = pltpu.get_barrier_semaphore()
    for step in STEPS:

        @pl.when(direct(step))
        def _():
            pl.semaphore_signal(barrier, inc=1, device_id=device(step), device_id_type=MESH)

    loads = [
        pltpu.make_async_copy(source, target, load_sems.at[index])
        for index, (source, target) in enumerate(
            ((material_in, material), (layers_in, layers), (volume_in, volume), (disp_in, disp))
        )
    ]
    for copy in loads:
        copy.start()

    lane = lax.broadcasted_iota(jnp.int32, (SUB, LANES), 1)
    sub_f = lax.broadcasted_iota(jnp.int32, (SUB, LANES), 0).astype(jnp.float32)
    zero = jnp.zeros((SUB, LANES), jnp.float32)

    def clear(ref, *where):
        ref[where] = jnp.zeros(ref.at[where].shape, jnp.float32)

    @pl.when(gy == 0)
    def _():
        clear(vol_ext, slice(0, WIDE), slice(left, right))
        clear(got_y, 0)

    @pl.when(gy == ny - 1)
    def _():
        clear(vol_ext, slice(bottom, bottom + WIDE), slice(left, right))
        clear(got_y, 1)

    for side, delta in enumerate(SIDES):

        @pl.when(jnp.logical_not(has((delta, 0))))
        def _():
            clear(got_xv, side)
            clear(got_x, side)

        @pl.when(jnp.logical_not(has((delta, 0)) & paired))
        def _():
            clear(via_xv, side)
            clear(via_x, side)

    for index, step in enumerate(CORNERS):

        @pl.when(jnp.logical_not(has(step)))
        def _():
            clear(got_cn, index)
            clear(got_cf, index)
            clear(got_c, index)

    for copy in loads[:3]:
        copy.wait()
    eye_row = lax.broadcasted_iota(jnp.int32, (cols, cols), 0)
    eye_col = lax.broadcasted_iota(jnp.int32, (cols, cols), 1)
    level = lax.broadcasted_iota(jnp.int32, (cols, LANES), 1).astype(jnp.float32)
    filled = jnp.where(material[...] > 0, layers[...], 0).astype(jnp.float32)
    for y in range(rows):
        line = jnp.broadcast_to(filled[y : y + 1, :], (cols, cols))
        top = jnp.sum(jnp.where(eye_row == eye_col, line, 0.0), axis=1, keepdims=True)
        vol_ext[WIDE + y, left:right, :] = jnp.where(
            level < jnp.broadcast_to(top, (cols, LANES)), volume[y], 0.0
        )

    def near_row(dy):
        return WIDE if dy < 0 else bottom - HORIZON

    def far_row(dy):
        return WIDE + HORIZON if dy < 0 else bottom - WIDE

    def near_halo(dy):
        return HORIZON if dy < 0 else bottom

    def far_halo(dy):
        return 0 if dy < 0 else bottom + HORIZON

    loads[3].wait()
    for side, delta in enumerate(SIDES):
        first = left if delta < 0 else right - WIDE
        for y in range(rows):
            send_xv[side, y * WIDE : (y + 1) * WIDE, :] = vol_ext[WIDE + y, first : first + WIDE, :]
        first = 0 if delta < 0 else cols - HORIZON
        for k in range(3):
            for y in range(rows):
                at = (k * rows + y) * HORIZON
                send_x[side, at : at + HORIZON, :] = disp[k, y, first : first + HORIZON, :]
    for index, (dx, dy) in enumerate(CORNERS):
        first = left if dx < 0 else right - WIDE
        for buffer, start in ((send_cn, near_row(dy)), (send_cf, far_row(dy))):
            for y in range(HORIZON):
                at = y * WIDE
                buffer[index, at : at + WIDE, :] = vol_ext[start + y, first : first + WIDE, :]
        first = 0 if dx < 0 else cols - HORIZON
        start = 0 if dy < 0 else rows - HORIZON
        for k in range(3):
            for y in range(HORIZON):
                at = (k * HORIZON + y) * HORIZON
                send_c[index, at : at + HORIZON, :] = disp[k, start + y, first : first + HORIZON, :]

    middle_x = left + cols // 2
    middle_y = HORIZON + rows // 2

    def place(k, value, y, at):
        width = value.shape[0]
        if k == 0:
            value = value + (sub_f[:width] + float(at - middle_x))
        if k == 1:
            value = value + (y - middle_y).astype(jnp.float32)
        ext[k, y, at : at + width, :] = value

    def own_row(y, carry):
        for at in range(0, cols, SUB):
            for k in range(3):
                place(k, disp[k, y, at : at + SUB, :], y + HORIZON, left + at)
                value = ext[k, y + HORIZON, left + at : left + at + SUB, :]
                for oz in AWAY:
                    there = moved(value, -oz)
                    if k == 2:
                        there = there - float(oz)
                    mine[k, AWAY.index(oz), y, left + at : left + at + SUB, :] = there
        return carry

    lax.fori_loop(0, rows, own_row, 0)

    peers = sum(direct(step).astype(jnp.int32) for step in STEPS)
    pl.semaphore_wait(barrier, peers)

    def cut_from(delta, size, width):
        return {-1: (0, width), 0: (0, size), 1: (size - width, width)}[delta]

    def vol_copy(step):
        return rows_copy(step, near_row, near_halo, send_cn, got_cn, 0)

    def far_copy(step):
        return rows_copy(step, far_row, far_halo, send_cf, got_cf, 4)

    def rows_copy(step, own, halo, send_corner, got_corner, sem):
        dx, dy = step
        if dx == 0:
            source = vol_ext.at[own(dy) : own(dy) + HORIZON, left:right]
            target = vol_ext.at[halo(-dy) : halo(-dy) + HORIZON, left:right]
        elif dy == 0:
            source, target = send_xv.at[0 if dx < 0 else 1], got_xv.at[0 if dx > 0 else 1]
        else:
            source = send_corner.at[CORNERS.index(step)]
            target = got_corner.at[CORNERS.index((-dx, -dy))]
        return pltpu.make_async_remote_copy(
            src_ref=source,
            dst_ref=target,
            send_sem=sems.at[sem, STEPS.index(step)],
            recv_sem=sems.at[sem + 1, STEPS.index((-dx, -dy))],
            device_id=device(step),
            device_id_type=MESH,
        )

    def via_copy(kind, side):
        source, target = ((got_xv, via_xv), (got_x, via_x))[kind]
        return pltpu.make_async_remote_copy(
            src_ref=source.at[side],
            dst_ref=target.at[side],
            send_sem=via_sems.at[2 * kind, side],
            recv_sem=via_sems.at[2 * kind + 1, side],
            device_id={"gx": gx, "gy": gy + toward},
            device_id_type=MESH,
        )

    def hand_on(kind):
        for side, delta in enumerate(SIDES):

            @pl.when(has((delta, 0)) & paired)
            def _():
                via_copy(kind, side).start()

    def handed(kind):
        for side, delta in enumerate(SIDES):

            @pl.when(has((delta, 0)) & paired)
            def _():
                via_copy(kind, side).wait_recv()

    def disp_copy(step):
        dx, dy = step
        if dx == 0:
            y0, yn = cut_from(dy, rows, HORIZON)
            source, target = disp.at[:, y0 : y0 + yn], got_y.at[0 if dy > 0 else 1]
        elif dy == 0:
            source, target = send_x.at[0 if dx < 0 else 1], got_x.at[0 if dx > 0 else 1]
        else:
            source, target = send_c.at[CORNERS.index(step)], got_c.at[CORNERS.index((-dx, -dy))]
        return pltpu.make_async_remote_copy(
            src_ref=source,
            dst_ref=target,
            send_sem=sems.at[2, STEPS.index(step)],
            recv_sem=sems.at[3, STEPS.index((-dx, -dy))],
            device_id=device(step),
            device_id_type=MESH,
        )

    along_x = [step for step in STEPS if step[1] == 0]
    along_y = [step for step in STEPS if step[0] == 0]
    sends = [(vol_copy, step) for step in (*along_y, *along_x, *CORNERS)]
    sends += [(disp_copy, step) for step in along_x]
    sends += [(far_copy, step) for step in (*CORNERS, *along_y)]
    sends += [(disp_copy, step) for step in (*CORNERS, *along_y)]
    for make, step in sends:

        @pl.when(direct(step))
        def _():
            make(step).start()

    def arrived(make, step):
        @pl.when(direct(step))
        def _():
            dx, dy = step
            make((-dx, -dy)).wait_recv()

    def fill_corners(buffer, row_there, row_here):
        for index, (dx, dy) in enumerate(CORNERS):
            side = 0 if dx < 0 else 1
            first = left - WIDE if dx < 0 else right
            there, here = row_there(-dy) - WIDE, row_here(dy)

            @pl.when(to_partner(dy))
            def _():
                for y in range(HORIZON):
                    at = (there + y) * WIDE
                    vol_ext[here + y, first : first + WIDE, :] = via_xv[side, at : at + WIDE, :]

            @pl.when(jnp.logical_not(to_partner(dy)))
            def _():
                for y in range(HORIZON):
                    at = y * WIDE
                    vol_ext[here + y, first : first + WIDE, :] = buffer[index, at : at + WIDE, :]

    bulk = math.pi * HORIZON**4 / 30.0
    near_rows = ext.shape[1]
    near_tiles = -(-(cols + 2 * HORIZON) // SUB)

    def factor_tile(y, at):
        row = y + HORIZON
        beside = {}
        for ax in range(HORIZON + 1):
            for ay in range(HORIZON + 1):
                if ax * ax + ay * ay > HORIZON * HORIZON:
                    continue
                total = None
                for dy in sorted({ay, -ay}):
                    for dx in sorted({ax, -ax}):
                        term = vol_ext[row + dy, at + dx : at + dx + SUB, :]
                        total = term if total is None else total + term
                beside[ax, ay] = total
        energy = [None, None, None]
        for k in range(3):
            for az in range(HORIZON + 1):
                layer = None
                for (ax, ay), total in beside.items():
                    square = ax * ax + ay * ay + az * az
                    part = (ax, ay, az)[k]
                    if not 0 < square <= HORIZON * HORIZON or not part:
                        continue
                    term = (influence(square) * part**4 / math.sqrt(square) ** 3) * total
                    layer = term if layer is None else layer + term
                if layer is None:
                    continue
                if az:
                    ahead = jnp.where(inside(lane, az), moved(layer, az), 0.0)
                    layer = ahead + jnp.where(inside(lane, -az), moved(layer, -az), 0.0)
                energy[k] = layer if energy[k] is None else energy[k] + layer
        alive = vol_ext[row, at : at + SUB, :] > 0
        for k in range(3):
            safe = jnp.where(alive, energy[k], 1.0)
            ext[3 + k, y, at : at + SUB, :] = jnp.where(alive, bulk / safe, 1.0)

    def factor_rows(first, step, stride, count, tiles):
        def body(i, carry):
            for y in range(count):
                for tile in tiles:
                    factor_tile(i * stride + first + y * step, left - HORIZON + tile * SUB)
            return carry

        return body

    def factor_moved(tiles):
        def body(i, carry):
            for part in range(4):
                y = i * 4 + part
                for tile in tiles:
                    at = left + tile * SUB
                    for k in range(3):
                        value = ext[3 + k, y + HORIZON, at : at + SUB, :]
                        for oz in AWAY:
                            if k == 2 or abs(oz) < HORIZON:
                                there = moved(value, -oz)
                                mine[3 + k, AWAY.index(oz), y, at : at + SUB, :] = there
            return carry

        return body

    def own_factors(near, own):
        lax.fori_loop(0, rows // 4, factor_rows(HORIZON, 1, 4, 4, near), 0)
        lax.fori_loop(0, rows // 4, factor_moved(own), 0)

    own_tiles = cols // SUB

    def middle():
        for step in along_y:
            arrived(vol_copy, step)
        own_factors(range(1, near_tiles - 1), range(1, own_tiles - 1))

    def edges():
        for step in along_x:
            arrived(vol_copy, step)
        hand_on(0)
        for side in range(2):
            first = left - WIDE if side == 0 else right
            for y in range(rows):
                at = y * WIDE
                vol_ext[WIDE + y, first : first + WIDE, :] = got_xv[side, at : at + WIDE, :]
        for step in CORNERS:
            arrived(vol_copy, step)
        handed(0)
        fill_corners(got_cn, near_row, near_halo)
        own_factors((0, near_tiles - 1), (0, own_tiles - 1))
        for step in along_x:
            arrived(disp_copy, step)
        hand_on(1)
        for side, at in ((0, left - HORIZON), (1, right)):

            def edge_row(y, carry):
                for k in range(3):
                    value = got_x[side, pl.ds((k * rows + y) * HORIZON, HORIZON), :]
                    place(k, value, y + HORIZON, at)
                return carry

            lax.fori_loop(0, rows, edge_row, 0)

    def halo_rows(side):
        delta = SIDES[side]
        base = 0 if side == 0 else HORIZON + rows

        def halo_row(y, carry):
            row = y + base
            for k in range(3):
                for at in range(0, cols, SUB):
                    place(k, got_y[side, k, y, at : at + SUB, :], row, left + at)
                for dx, at in ((-1, left - HORIZON), (1, right)):
                    corner = CORNERS.index((dx, delta))
                    there = y if delta > 0 else y + (rows - HORIZON)

                    @pl.when(to_partner(delta))
                    def _():
                        from_via = pl.ds((k * rows + there) * HORIZON, HORIZON)
                        place(k, via_x[0 if dx < 0 else 1, from_via, :], row, at)

                    @pl.when(jnp.logical_not(to_partner(delta)))
                    def _():
                        from_corner = pl.ds((k * HORIZON + y) * HORIZON, HORIZON)
                        place(k, got_c[corner, from_corner, :], row, at)

            return carry

        lax.fori_loop(0, HORIZON, halo_row, 0)

    early = rows - 2 * HORIZON
    inner = own_tiles - 2

    def tile_step(i, carry):
        @pl.when(i == early * inner)
        def _():
            edges()

        later = i - early * inner
        slot = jnp.where(later < 0, lax.div(i, inner), lax.div(later, 2))
        tile = jnp.where(later < 0, lax.rem(i, inner) + 1, lax.rem(later, 2) * (own_tiles - 1))
        force_tile(vol_ext, ext, mine, sums, middle_row(rows, slot), slot, tile)
        return carry

    middle()
    lax.fori_loop(0, early * own_tiles, tile_step, 0)
    for step in (*CORNERS, *along_y):
        arrived(far_copy, step)
    fill_corners(got_cf, far_row, far_halo)
    lax.fori_loop(0, HORIZON, factor_rows(0, rows + HORIZON, 1, 2, range(near_tiles)), 0)
    for step in (*CORNERS, *along_y):
        arrived(disp_copy, step)
    handed(1)
    for side in (1, 0):
        halo_rows(side)

    for make, step in sends:

        @pl.when(direct(step))
        def _():
            make(step).wait_send()

    for side, delta in enumerate(SIDES):

        @pl.when(has((delta, 0)) & paired)
        def _():
            for kind in range(2):
                via_copy(kind, side).wait_send()


def rest(
    vol_ext, ext, mine, early, fac_out, force_out, sums, force, out_sems, fac_sem
):
    rows, cols = force.shape[1], force.shape[2]
    lane = lax.broadcasted_iota(jnp.int32, (SUB, LANES), 1)
    own = ext.at[3:6, HORIZON : HORIZON + rows, SUB : SUB + cols]
    fac_copy = pltpu.make_async_copy(own, fac_out, fac_sem)
    fac_copy.start()
    done = early.shape[2]
    half = sums.shape[2]

    def out_copy(y):
        return pltpu.make_async_copy(force.at[:, y], force_out.at[:, y], out_sems.at[y])

    def finish(parts, slot, y):
        for at in range(0, cols, SUB):
            alive = vol_ext[y + WIDE, SUB + at : 2 * SUB + at, :] > 0
            for k in range(3):
                total = parts[k, HORIZON, slot, at : at + SUB, :]
                for oz in AWAY:
                    part = moved(parts[k, oz + HORIZON, slot, at : at + SUB, :], oz)
                    total = total + jnp.where(inside(lane, oz), part, 0.0)
                force[k, y, at : at + SUB, :] = jnp.where(alive, total, 0.0)
        out_copy(y).start()

    def group(first, carry):
        def row(slot, inner):
            y = middle_row(rows, first * half + slot + done)

            def one(tile, last):
                force_tile(vol_ext, ext, mine, sums, y, slot, tile)
                return last

            return lax.fori_loop(0, cols // SUB, one, inner)

        lax.fori_loop(0, half, row, 0)
        for slot in range(half):
            finish(sums, slot, middle_row(rows, first * half + slot + done))
        return carry

    for slot in range(done):
        finish(early, slot, (slot + HORIZON) % rows)
    lax.fori_loop(0, (rows - done) // half, group, 0)
    fac_copy.wait()
    for y in range(rows):
        out_copy(y).wait()


def shards(displacement, volume, material, layers):
    _, rows, cols, depth = displacement.shape
    wide_rows, wide_cols = rows + 2 * WIDE, cols + 2 * SUB
    near_rows = rows + 2 * HORIZON
    hbm = pl.BlockSpec(memory_space=pltpu.MemorySpace.HBM)
    result = jax.ShapeDtypeStruct((3, rows, cols, depth), jnp.float32)

    def whole(count):
        return -(-count // SUB) * SUB

    edge, corner = whole(3 * rows * HORIZON), whole(3 * HORIZON * HORIZON)
    edge_vol, corner_vol = whole(rows * WIDE), whole(HORIZON * WIDE)

    def scratch(*shape):
        return pltpu.VMEM(shape + (depth,), jnp.float32)

    def held(*shape):
        return pltpu.VMEM(shape + (depth,), jnp.float32)

    def pin(values, space):
        return [pltpu.with_memory_space_constraint(value, space) for value in values]

    vmem = pl.BlockSpec(memory_space=pltpu.VMEM)
    early = rows - 2 * HORIZON
    frames = 2 * HORIZON + 1
    state = pl.pallas_call(
        kernel,
        out_shape=(
            held(wide_rows, wide_cols),
            held(6, near_rows, wide_cols),
            held(6, len(AWAY), rows, wide_cols),
            held(3, frames, early, cols),
        ),
        in_specs=[hbm] * 4,
        out_specs=(vmem,) * 4,
        scratch_shapes=[
            scratch(3, rows, cols),
            scratch(rows, cols),
            pltpu.VMEM((rows, cols), jnp.int32),
            pltpu.VMEM((rows, cols), jnp.int32),
            scratch(2, edge_vol),
            scratch(4, corner_vol),
            scratch(4, corner_vol),
            scratch(2, edge),
            scratch(4, corner),
            scratch(2, edge_vol),
            scratch(4, corner_vol),
            scratch(4, corner_vol),
            scratch(2, 3, HORIZON, cols),
            scratch(2, edge),
            scratch(4, corner),
            scratch(2, edge_vol),
            scratch(2, edge),
            pltpu.SemaphoreType.DMA((6, len(STEPS))),
            pltpu.SemaphoreType.DMA((4, 2)),
            pltpu.SemaphoreType.DMA((4,)),
        ],
        compiler_params=pltpu.CompilerParams(
            collective_id=0, has_side_effects=True, vmem_limit_bytes=VMEM_LIMIT
        ),
        name="gather",
    )(*pin((displacement, volume, material, layers), pltpu.MemorySpace.HBM))
    return pl.pallas_call(
        rest,
        out_shape=(result, result),
        in_specs=[vmem] * 4,
        out_specs=(hbm, hbm),
        scratch_shapes=[
            scratch(3, frames, HORIZON, cols),
            scratch(3, rows, cols),
            pltpu.SemaphoreType.DMA((rows,)),
            pltpu.SemaphoreType.DMA,
        ],
        compiler_params=pltpu.CompilerParams(vmem_limit_bytes=VMEM_LIMIT),
        name="rest",
    )(*pin(state, pltpu.MemorySpace.VMEM))


def solution(mesh):
    return jax.shard_map(
        shards,
        mesh=mesh,
        in_specs=(P(None, "gy", "gx", None), P("gy", "gx", None), P("gy", "gx"), P("gy", "gx")),
        out_specs=(P(None, "gy", "gx", None), P(None, "gy", "gx", None)),
        check_vma=False,
    )
```

```python
import math

import jax
import jax.numpy as jnp
from jax import lax
from jax.experimental import pallas as pl
from jax.experimental.pallas import tpu as pltpu
from jax.sharding import PartitionSpec as P

HORIZON = 3
STIFF = 5.0
WIDE = 2 * HORIZON
LANES = 128
VMEM_LIMIT = 24 * 2**20
SUB = 8
MESH = pl.DeviceIdType.MESH
SIDES = (-1, 1)
STEPS = tuple((dx, dy) for dy in (-1, 0, 1) for dx in (-1, 0, 1) if (dx, dy) != (0, 0))
CORNERS = tuple(step for step in STEPS if step[0] and step[1])


def bond_list():
    reach = range(-HORIZON, HORIZON + 1)
    return [
        (x, y, z)
        for y in reach
        for x in reach
        for z in reach
        if 0 < x * x + y * y + z * z <= HORIZON * HORIZON
    ]


def bond_types(oz):
    kinds = {}
    for bond in bond_list():
        if bond[2] == oz:
            kinds.setdefault(tuple(sorted(map(abs, bond))), []).append(bond)
    return kinds


def influence(square):
    return (1.0 - square / (HORIZON * HORIZON)) ** 2


AWAY = tuple(oz for oz in range(-HORIZON, HORIZON + 1) if oz)


def moved(value, step):
    return pltpu.roll(value, (-step) % LANES, 1) if step else value


def inside(lane, step):
    return lane < LANES - step if step > 0 else lane >= -step


def middle_row(rows, index):
    return lax.rem(index + HORIZON, rows)


def known_bonds():
    return [bond for bond in bond_list() if abs(bond[1]) < HORIZON]


def bond_scale(kind):
    square = sum(a * a for a in kind)
    length = math.sqrt(square)
    scale = 0.5 if sum(a > 0 for a in kind) == 1 else length / (2.0 * math.gcd(*kind))
    return STIFF * influence(square) * scale, length


def stretch_tile(vol_ext, ext, mine, known, y, slot, tile):
    start = pl.multiple_of(tile * SUB, SUB)
    row = y + HORIZON
    own = {}
    for index, bond in enumerate(known_bonds()):
        ox, oy, oz = bond
        at = pl.ds(start + (SUB + ox), SUB)
        apart = []
        for k in range(3):
            if (k, oz) not in own:
                if oz:
                    own[k, oz] = mine[k, AWAY.index(oz), y, pl.ds(start + SUB, SUB), :]
                else:
                    own[k, oz] = ext[k, row, pl.ds(start + SUB, SUB), :]
            apart.append(ext[k, row + oy, at, :] - own[k, oz])
        squared = apart[0] * apart[0] + apart[1] * apart[1] + apart[2] * apart[2]
        scale, length = bond_scale(tuple(sorted(map(abs, bond))))
        pull = scale / length - scale * lax.rsqrt(squared)
        pull = pull * vol_ext[row + HORIZON + oy, at, :]
        for k in range(3):
            known[slot, index, k] = pull * apart[k]


def force_tile(vol_ext, ext, mine, sums, y, slot, tile, known=None, place=None):
    start = pl.multiple_of(tile * SUB, SUB)
    row = y + HORIZON
    stored = known_bonds()

    def load(field, ox, oy):
        at = pl.ds(start + (SUB + ox), SUB)
        if field == 6:
            return vol_ext[row + HORIZON + oy, at, :]
        return ext[field, row + oy, at, :]

    for oz in sorted(range(-HORIZON, HORIZON + 1), key=abs):
        kinds = bond_types(oz)
        own = {}
        for f in range(6):
            if oz == 0:
                own[f] = load(f, 0, 0)
            elif f < 3 or f == 5 or abs(oz) < HORIZON:
                own[f] = mine[f, AWAY.index(oz), y, pl.ds(start + SUB, SUB), :]
        summed = [None, None, None]

        def add(sums, factor, values):
            for k in range(3):
                term = factor * values[k]
                sums[k] = term if sums[k] is None else sums[k] + term

        for kind, bonds in kinds.items():
            scale, length = bond_scale(kind)
            common = math.gcd(*kind)
            count = sum(a > 0 for a in kind)
            late = len(bonds) > 6 and known is None
            total = [None, None, None]
            for bond in bonds:
                ox, oy, _ = bond
                near = [k for k in range(3) if bond[k]]
                pair = {k: own[3 + k] + load(3 + k, ox, oy) for k in near}
                if count == 1:
                    ratio = pair[near[0]]
                else:
                    two = {k: pair[k] * pair[k] for k in near}
                    part = {k: (bond[k] // common) ** 2 for k in near}
                    if count == 2:
                        a, b = near
                        first = two[b] if part[a] == 1 else two[b] * float(part[a])
                        second = two[a] if part[b] == 1 else two[a] * float(part[b])
                        ratio = pair[a] * pair[b] * lax.rsqrt(first + second)
                    else:
                        odd = next(
                            k for k in near if sum(part[j] == part[k] for j in near) in (1, 3)
                        )
                        a, b = [k for k in near if k != odd]
                        first = two[a] * two[b]
                        if part[odd] != 1:
                            first = first * float(part[odd])
                        second = two[odd] * (two[a] + two[b])
                        if part[a] != 1:
                            second = second * float(part[a])
                        ratio = pair[a] * pair[b] * pair[odd] * lax.rsqrt(first + second)
                if known is not None and bond in stored:
                    index = stored.index(bond)
                    add(summed, ratio, [known[place, index, k] for k in range(3)])
                    continue
                apart = [load(k, ox, oy) - own[k] for k in range(3)]
                squared = apart[0] * apart[0] + apart[1] * apart[1] + apart[2] * apart[2]
                if late:
                    pull = 1.0 / length - lax.rsqrt(squared)
                else:
                    pull = scale / length - scale * lax.rsqrt(squared)
                factor = (ratio * pull) * load(6, ox, oy)
                add(total if late else summed, factor, apart)
            if late:
                add(summed, scale, total)
        for k in range(3):
            sums[k, oz + HORIZON, slot, pl.ds(start, SUB), :] = summed[k]


def kernel(
    disp_in, volume_in, material_in, layers_in, vol_ext, ext, mine, sums, known,
    disp, volume, material, layers,
    send_xv, send_cn, send_cf, send_x, send_c, got_xv, got_cn, got_cf, got_y, got_x, got_c,
    via_xv, via_x, sems, via_sems, load_sems,
):
    rows, cols = volume.shape[0], volume.shape[1]
    left = SUB
    right = left + cols
    bottom = WIDE + rows
    gx, gy = lax.axis_index("gx"), lax.axis_index("gy")
    nx, ny = lax.axis_size("gx"), lax.axis_size("gy")

    def has(step):
        dx, dy = step
        found = None
        for delta, at, size in ((dx, gx, nx), (dy, gy, ny)):
            if delta:
                test = at > 0 if delta < 0 else at < size - 1
                found = test if found is None else found & test
        return found

    odd = lax.rem(gy, 2)
    toward = 1 - 2 * odd
    paired = (gy + toward >= 0) & (gy + toward < ny)

    def to_partner(dy):
        return odd == (1 if dy < 0 else 0)

    def direct(step):
        if step in CORNERS:
            return has(step) & jnp.logical_not(to_partner(step[1]))
        return has(step)

    def device(step):
        return {"gx": gx + step[0], "gy": gy + step[1]}

    barrier = pltpu.get_barrier_semaphore()
    for step in STEPS:

        @pl.when(direct(step))
        def _():
            pl.semaphore_signal(barrier, inc=1, device_id=device(step), device_id_type=MESH)

    loads = [
        pltpu.make_async_copy(source, target, load_sems.at[index])
        for index, (source, target) in enumerate(
            ((material_in, material), (layers_in, layers), (volume_in, volume), (disp_in, disp))
        )
    ]
    for copy in loads:
        copy.start()

    lane = lax.broadcasted_iota(jnp.int32, (SUB, LANES), 1)
    sub_f = lax.broadcasted_iota(jnp.int32, (SUB, LANES), 0).astype(jnp.float32)
    zero = jnp.zeros((SUB, LANES), jnp.float32)

    def clear(ref, *where):
        ref[where] = jnp.zeros(ref.at[where].shape, jnp.float32)

    @pl.when(gy == 0)
    def _():
        clear(vol_ext, slice(0, WIDE), slice(left, right))
        clear(got_y, 0)

    @pl.when(gy == ny - 1)
    def _():
        clear(vol_ext, slice(bottom, bottom + WIDE), slice(left, right))
        clear(got_y, 1)

    for side, delta in enumerate(SIDES):

        @pl.when(jnp.logical_not(has((delta, 0))))
        def _():
            clear(got_xv, side)
            clear(got_x, side)

        @pl.when(jnp.logical_not(has((delta, 0)) & paired))
        def _():
            clear(via_xv, side)
            clear(via_x, side)

    for index, step in enumerate(CORNERS):

        @pl.when(jnp.logical_not(has(step)))
        def _():
            clear(got_cn, index)
            clear(got_cf, index)
            clear(got_c, index)

    for copy in loads[:3]:
        copy.wait()
    eye_row = lax.broadcasted_iota(jnp.int32, (cols, cols), 0)
    eye_col = lax.broadcasted_iota(jnp.int32, (cols, cols), 1)
    level = lax.broadcasted_iota(jnp.int32, (cols, LANES), 1).astype(jnp.float32)
    filled = jnp.where(material[...] > 0, layers[...], 0).astype(jnp.float32)
    for y in range(rows):
        line = jnp.broadcast_to(filled[y : y + 1, :], (cols, cols))
        top = jnp.sum(jnp.where(eye_row == eye_col, line, 0.0), axis=1, keepdims=True)
        vol_ext[WIDE + y, left:right, :] = jnp.where(
            level < jnp.broadcast_to(top, (cols, LANES)), volume[y], 0.0
        )

    def near_row(dy):
        return WIDE if dy < 0 else bottom - HORIZON

    def far_row(dy):
        return WIDE + HORIZON if dy < 0 else bottom - WIDE

    def near_halo(dy):
        return HORIZON if dy < 0 else bottom

    def far_halo(dy):
        return 0 if dy < 0 else bottom + HORIZON

    loads[3].wait()
    for side, delta in enumerate(SIDES):
        first = left if delta < 0 else right - WIDE
        for y in range(rows):
            send_xv[side, y * WIDE : (y + 1) * WIDE, :] = vol_ext[WIDE + y, first : first + WIDE, :]
        first = 0 if delta < 0 else cols - HORIZON
        for k in range(3):
            for y in range(rows):
                at = (k * rows + y) * HORIZON
                send_x[side, at : at + HORIZON, :] = disp[k, y, first : first + HORIZON, :]
    for index, (dx, dy) in enumerate(CORNERS):
        first = left if dx < 0 else right - WIDE
        for buffer, start in ((send_cn, near_row(dy)), (send_cf, far_row(dy))):
            for y in range(HORIZON):
                at = y * WIDE
                buffer[index, at : at + WIDE, :] = vol_ext[start + y, first : first + WIDE, :]
        first = 0 if dx < 0 else cols - HORIZON
        start = 0 if dy < 0 else rows - HORIZON
        for k in range(3):
            for y in range(HORIZON):
                at = (k * HORIZON + y) * HORIZON
                send_c[index, at : at + HORIZON, :] = disp[k, start + y, first : first + HORIZON, :]

    middle_x = left + cols // 2
    middle_y = HORIZON + rows // 2

    def place(k, value, y, at):
        width = value.shape[0]
        if k == 0:
            value = value + (sub_f[:width] + float(at - middle_x))
        if k == 1:
            value = value + (y - middle_y).astype(jnp.float32)
        ext[k, y, at : at + width, :] = value

    def own_row(y, carry):
        for at in range(0, cols, SUB):
            for k in range(3):
                place(k, disp[k, y, at : at + SUB, :], y + HORIZON, left + at)
                value = ext[k, y + HORIZON, left + at : left + at + SUB, :]
                for oz in AWAY:
                    there = moved(value, -oz)
                    if k == 2:
                        there = there - float(oz)
                    mine[k, AWAY.index(oz), y, left + at : left + at + SUB, :] = there
        return carry

    lax.fori_loop(0, rows, own_row, 0)

    peers = sum(direct(step).astype(jnp.int32) for step in STEPS)
    pl.semaphore_wait(barrier, peers)

    def cut_from(delta, size, width):
        return {-1: (0, width), 0: (0, size), 1: (size - width, width)}[delta]

    def vol_copy(step):
        return rows_copy(step, near_row, near_halo, send_cn, got_cn, 0)

    def far_copy(step):
        return rows_copy(step, far_row, far_halo, send_cf, got_cf, 4)

    def rows_copy(step, own, halo, send_corner, got_corner, sem):
        dx, dy = step
        if dx == 0:
            source = vol_ext.at[own(dy) : own(dy) + HORIZON, left:right]
            target = vol_ext.at[halo(-dy) : halo(-dy) + HORIZON, left:right]
        elif dy == 0:
            source, target = send_xv.at[0 if dx < 0 else 1], got_xv.at[0 if dx > 0 else 1]
        else:
            source = send_corner.at[CORNERS.index(step)]
            target = got_corner.at[CORNERS.index((-dx, -dy))]
        return pltpu.make_async_remote_copy(
            src_ref=source,
            dst_ref=target,
            send_sem=sems.at[sem, STEPS.index(step)],
            recv_sem=sems.at[sem + 1, STEPS.index((-dx, -dy))],
            device_id=device(step),
            device_id_type=MESH,
        )

    def via_copy(kind, side):
        source, target = ((got_xv, via_xv), (got_x, via_x))[kind]
        return pltpu.make_async_remote_copy(
            src_ref=source.at[side],
            dst_ref=target.at[side],
            send_sem=via_sems.at[2 * kind, side],
            recv_sem=via_sems.at[2 * kind + 1, side],
            device_id={"gx": gx, "gy": gy + toward},
            device_id_type=MESH,
        )

    def hand_on(kind):
        for side, delta in enumerate(SIDES):

            @pl.when(has((delta, 0)) & paired)
            def _():
                via_copy(kind, side).start()

    def handed(kind):
        for side, delta in enumerate(SIDES):

            @pl.when(has((delta, 0)) & paired)
            def _():
                via_copy(kind, side).wait_recv()

    def disp_copy(step):
        dx, dy = step
        if dx == 0:
            y0, yn = cut_from(dy, rows, HORIZON)
            source, target = disp.at[:, y0 : y0 + yn], got_y.at[0 if dy > 0 else 1]
        elif dy == 0:
            source, target = send_x.at[0 if dx < 0 else 1], got_x.at[0 if dx > 0 else 1]
        else:
            source, target = send_c.at[CORNERS.index(step)], got_c.at[CORNERS.index((-dx, -dy))]
        return pltpu.make_async_remote_copy(
            src_ref=source,
            dst_ref=target,
            send_sem=sems.at[2, STEPS.index(step)],
            recv_sem=sems.at[3, STEPS.index((-dx, -dy))],
            device_id=device(step),
            device_id_type=MESH,
        )

    along_x = [step for step in STEPS if step[1] == 0]
    along_y = [step for step in STEPS if step[0] == 0]
    sends = [(vol_copy, step) for step in (*along_y, *along_x, *CORNERS)]
    sends += [(disp_copy, step) for step in along_x]
    sends += [(far_copy, step) for step in (*CORNERS, *along_y)]
    sends += [(disp_copy, step) for step in (*CORNERS, *along_y)]
    for make, step in sends:

        @pl.when(direct(step))
        def _():
            make(step).start()

    def arrived(make, step):
        @pl.when(direct(step))
        def _():
            dx, dy = step
            make((-dx, -dy)).wait_recv()

    def fill_corners(buffer, row_there, row_here):
        for index, (dx, dy) in enumerate(CORNERS):
            side = 0 if dx < 0 else 1
            first = left - WIDE if dx < 0 else right
            there, here = row_there(-dy) - WIDE, row_here(dy)

            @pl.when(to_partner(dy))
            def _():
                for y in range(HORIZON):
                    at = (there + y) * WIDE
                    vol_ext[here + y, first : first + WIDE, :] = via_xv[side, at : at + WIDE, :]

            @pl.when(jnp.logical_not(to_partner(dy)))
            def _():
                for y in range(HORIZON):
                    at = y * WIDE
                    vol_ext[here + y, first : first + WIDE, :] = buffer[index, at : at + WIDE, :]

    bulk = math.pi * HORIZON**4 / 30.0
    near_rows = ext.shape[1]
    near_tiles = -(-(cols + 2 * HORIZON) // SUB)

    def factor_tile(y, at):
        row = y + HORIZON
        beside = {}
        for ax in range(HORIZON + 1):
            for ay in range(HORIZON + 1):
                if ax * ax + ay * ay > HORIZON * HORIZON:
                    continue
                total = None
                for dy in sorted({ay, -ay}):
                    for dx in sorted({ax, -ax}):
                        term = vol_ext[row + dy, at + dx : at + dx + SUB, :]
                        total = term if total is None else total + term
                beside[ax, ay] = total
        energy = [None, None, None]
        for k in range(3):
            for az in range(HORIZON + 1):
                layer = None
                for (ax, ay), total in beside.items():
                    square = ax * ax + ay * ay + az * az
                    part = (ax, ay, az)[k]
                    if not 0 < square <= HORIZON * HORIZON or not part:
                        continue
                    term = (influence(square) * part**4 / math.sqrt(square) ** 3) * total
                    layer = term if layer is None else layer + term
                if layer is None:
                    continue
                if az:
                    ahead = jnp.where(inside(lane, az), moved(layer, az), 0.0)
                    layer = ahead + jnp.where(inside(lane, -az), moved(layer, -az), 0.0)
                energy[k] = layer if energy[k] is None else energy[k] + layer
        alive = vol_ext[row, at : at + SUB, :] > 0
        for k in range(3):
            safe = jnp.where(alive, energy[k], 1.0)
            ext[3 + k, y, at : at + SUB, :] = jnp.where(alive, bulk / safe, 1.0)

    def factor_rows(first, step, stride, count, tiles):
        def body(i, carry):
            for y in range(count):
                for tile in tiles:
                    factor_tile(i * stride + first + y * step, left - HORIZON + tile * SUB)
            return carry

        return body

    def factor_moved(tiles):
        def body(i, carry):
            for part in range(4):
                y = i * 4 + part
                for tile in tiles:
                    at = left + tile * SUB
                    for k in range(3):
                        value = ext[3 + k, y + HORIZON, at : at + SUB, :]
                        for oz in AWAY:
                            if k == 2 or abs(oz) < HORIZON:
                                there = moved(value, -oz)
                                mine[3 + k, AWAY.index(oz), y, at : at + SUB, :] = there
            return carry

        return body

    def own_factors(near, own):
        lax.fori_loop(0, rows // 4, factor_rows(HORIZON, 1, 4, 4, near), 0)
        lax.fori_loop(0, rows // 4, factor_moved(own), 0)

    own_tiles = cols // SUB

    def middle():
        for step in along_y:
            arrived(vol_copy, step)
        own_factors(range(1, near_tiles - 1), range(1, own_tiles - 1))

    def edges():
        for step in along_x:
            arrived(vol_copy, step)
        hand_on(0)
        for side in range(2):
            first = left - WIDE if side == 0 else right
            for y in range(rows):
                at = y * WIDE
                vol_ext[WIDE + y, first : first + WIDE, :] = got_xv[side, at : at + WIDE, :]
        for step in CORNERS:
            arrived(vol_copy, step)
        handed(0)
        fill_corners(got_cn, near_row, near_halo)
        own_factors((0, near_tiles - 1), (0, own_tiles - 1))
        for step in along_x:
            arrived(disp_copy, step)
        hand_on(1)
        for side, at in ((0, left - HORIZON), (1, right)):

            def edge_row(y, carry):
                for k in range(3):
                    value = got_x[side, pl.ds((k * rows + y) * HORIZON, HORIZON), :]
                    place(k, value, y + HORIZON, at)
                return carry

            lax.fori_loop(0, rows, edge_row, 0)

    def halo_rows(side):
        delta = SIDES[side]
        base = 0 if side == 0 else HORIZON + rows

        def halo_row(y, carry):
            row = y + base
            for k in range(3):
                for at in range(0, cols, SUB):
                    place(k, got_y[side, k, y, at : at + SUB, :], row, left + at)
                for dx, at in ((-1, left - HORIZON), (1, right)):
                    corner = CORNERS.index((dx, delta))
                    there = y if delta > 0 else y + (rows - HORIZON)

                    @pl.when(to_partner(delta))
                    def _():
                        from_via = pl.ds((k * rows + there) * HORIZON, HORIZON)
                        place(k, via_x[0 if dx < 0 else 1, from_via, :], row, at)

                    @pl.when(jnp.logical_not(to_partner(delta)))
                    def _():
                        from_corner = pl.ds((k * HORIZON + y) * HORIZON, HORIZON)
                        place(k, got_c[corner, from_corner, :], row, at)

            return carry

        lax.fori_loop(0, HORIZON, halo_row, 0)

    early = rows - 2 * HORIZON
    inner = own_tiles - 2

    def stretch_step(i, carry):
        y = lax.div(i, inner) + (HORIZON - 1)
        stretch_tile(vol_ext, ext, mine, known, y, i, lax.rem(i, inner) + 1)
        return carry

    def middle_step(i, carry):
        slot = lax.div(i, inner)
        tile = lax.rem(i, inner) + 1
        y = slot + HORIZON
        force_tile(vol_ext, ext, mine, sums, y, slot, tile, known, i + inner)
        return carry

    def edge_step(i, carry):
        slot = lax.div(i, 2)
        tile = lax.rem(i, 2) * (own_tiles - 1)
        force_tile(vol_ext, ext, mine, sums, slot + HORIZON, slot, tile)
        return carry

    lax.fori_loop(0, (early + 2) * inner, stretch_step, 0)
    middle()
    lax.fori_loop(0, early * inner, middle_step, 0)
    edges()
    lax.fori_loop(0, early * 2, edge_step, 0)
    for step in (*CORNERS, *along_y):
        arrived(far_copy, step)
    fill_corners(got_cf, far_row, far_halo)
    lax.fori_loop(0, HORIZON, factor_rows(0, rows + HORIZON, 1, 2, range(near_tiles)), 0)
    for step in (*CORNERS, *along_y):
        arrived(disp_copy, step)
    handed(1)
    for side in (1, 0):
        halo_rows(side)

    for make, step in sends:

        @pl.when(direct(step))
        def _():
            make(step).wait_send()

    for side, delta in enumerate(SIDES):

        @pl.when(has((delta, 0)) & paired)
        def _():
            for kind in range(2):
                via_copy(kind, side).wait_send()


def rest(
    vol_ext, ext, mine, early, known, fac_out, force_out, sums, force, out_sems, fac_sem
):
    rows, cols = force.shape[1], force.shape[2]
    lane = lax.broadcasted_iota(jnp.int32, (SUB, LANES), 1)
    own = ext.at[3:6, HORIZON : HORIZON + rows, SUB : SUB + cols]
    fac_copy = pltpu.make_async_copy(own, fac_out, fac_sem)
    fac_copy.start()
    done = early.shape[2]
    count = sums.shape[2]
    half = count // 2
    each = (count * (cols // SUB) - 2 * (cols // SUB - 2)) // 2

    def out_copy(y):
        return pltpu.make_async_copy(force.at[:, y], force_out.at[:, y], out_sems.at[y])

    def finish(parts, slot, y):
        for at in range(0, cols, SUB):
            alive = vol_ext[y + WIDE, SUB + at : 2 * SUB + at, :] > 0
            for k in range(3):
                total = parts[k, HORIZON, slot, at : at + SUB, :]
                for oz in AWAY:
                    part = moved(parts[k, oz + HORIZON, slot, at : at + SUB, :], oz)
                    total = total + jnp.where(inside(lane, oz), part, 0.0)
                force[k, y, at : at + SUB, :] = jnp.where(alive, total, 0.0)
        out_copy(y).start()

    tiles = cols // SUB
    inner = tiles - 2

    def middle_step(i, carry):
        end = lax.div(i, inner)
        tile = lax.rem(i, inner)
        y = jnp.where(end == 0, HORIZON + done, HORIZON - 1)
        place = jnp.where(end == 0, (done + 1) * inner, 0) + tile
        force_tile(vol_ext, ext, mine, sums, y, end * (count - 1), tile + 1, known, place)
        return carry

    def group(part, carry):
        def step(j, last):
            i = part * each + j
            between = lax.rem(i + (tiles - 2), tiles)
            end = (i < 2) | (i >= 2 * each - 2)
            slot = lax.div(i + (tiles - 2), tiles)
            tile = jnp.where(end, lax.rem(i, 2) * (tiles - 1), between)
            force_tile(vol_ext, ext, mine, sums, middle_row(rows, slot + done), slot, tile)
            return last

        lax.fori_loop(0, each, step, carry)
        for slot in range(half):
            at = part * half + slot
            finish(sums, at, middle_row(rows, at + done))
        return carry

    for slot in range(done):
        finish(early, slot, (slot + HORIZON) % rows)
    lax.fori_loop(0, 2 * inner, middle_step, 0)
    lax.fori_loop(0, 2, group, 0)
    fac_copy.wait()
    for y in range(rows):
        out_copy(y).wait()


def shards(displacement, volume, material, layers):
    _, rows, cols, depth = displacement.shape
    wide_rows, wide_cols = rows + 2 * WIDE, cols + 2 * SUB
    near_rows = rows + 2 * HORIZON
    hbm = pl.BlockSpec(memory_space=pltpu.MemorySpace.HBM)
    result = jax.ShapeDtypeStruct((3, rows, cols, depth), jnp.float32)

    def whole(count):
        return -(-count // SUB) * SUB

    edge, corner = whole(3 * rows * HORIZON), whole(3 * HORIZON * HORIZON)
    edge_vol, corner_vol = whole(rows * WIDE), whole(HORIZON * WIDE)

    def scratch(*shape):
        return pltpu.VMEM(shape + (depth,), jnp.float32)

    def held(*shape):
        return pltpu.VMEM(shape + (depth,), jnp.float32)

    def pin(values, space):
        return [pltpu.with_memory_space_constraint(value, space) for value in values]

    vmem = pl.BlockSpec(memory_space=pltpu.VMEM)
    early = rows - 2 * HORIZON
    frames = 2 * HORIZON + 1
    state = pl.pallas_call(
        kernel,
        out_shape=(
            held(wide_rows, wide_cols),
            held(6, near_rows, wide_cols),
            held(6, len(AWAY), rows, wide_cols),
            held(3, frames, early, cols),
            held((early + 2) * (cols // SUB - 2), len(known_bonds()), 3, SUB),
        ),
        in_specs=[hbm] * 4,
        out_specs=(vmem,) * 5,
        scratch_shapes=[
            scratch(3, rows, cols),
            scratch(rows, cols),
            pltpu.VMEM((rows, cols), jnp.int32),
            pltpu.VMEM((rows, cols), jnp.int32),
            scratch(2, edge_vol),
            scratch(4, corner_vol),
            scratch(4, corner_vol),
            scratch(2, edge),
            scratch(4, corner),
            scratch(2, edge_vol),
            scratch(4, corner_vol),
            scratch(4, corner_vol),
            scratch(2, 3, HORIZON, cols),
            scratch(2, edge),
            scratch(4, corner),
            scratch(2, edge_vol),
            scratch(2, edge),
            pltpu.SemaphoreType.DMA((6, len(STEPS))),
            pltpu.SemaphoreType.DMA((4, 2)),
            pltpu.SemaphoreType.DMA((4,)),
        ],
        compiler_params=pltpu.CompilerParams(
            collective_id=0, has_side_effects=True, vmem_limit_bytes=VMEM_LIMIT
        ),
        name="gather",
    )(*pin((displacement, volume, material, layers), pltpu.MemorySpace.HBM))
    return pl.pallas_call(
        rest,
        out_shape=(result, result),
        in_specs=[vmem] * 5,
        out_specs=(hbm, hbm),
        scratch_shapes=[
            scratch(3, frames, rows - early, cols),
            scratch(3, rows, cols),
            pltpu.SemaphoreType.DMA((rows,)),
            pltpu.SemaphoreType.DMA,
        ],
        compiler_params=pltpu.CompilerParams(vmem_limit_bytes=VMEM_LIMIT),
        name="rest",
    )(*pin(state, pltpu.MemorySpace.VMEM))


def solution(mesh):
    return jax.shard_map(
        shards,
        mesh=mesh,
        in_specs=(P(None, "gy", "gx", None), P("gy", "gx", None), P("gy", "gx"), P("gy", "gx")),
        out_specs=(P(None, "gy", "gx", None), P(None, "gy", "gx", None)),
        check_vma=False,
    )
```

```python
import math

import jax
import jax.numpy as jnp
from jax import lax
from jax.experimental import pallas as pl
from jax.experimental.pallas import tpu as pltpu
from jax.sharding import PartitionSpec as P

HORIZON = 3
STIFF = 5.0
WIDE = 2 * HORIZON
LANES = 128
VMEM_LIMIT = 16 * 2**20
SUB = 8
MESH = pl.DeviceIdType.MESH
SIDES = (-1, 1)
STEPS = tuple((dx, dy) for dy in (-1, 0, 1) for dx in (-1, 0, 1) if (dx, dy) != (0, 0))
CORNERS = tuple(step for step in STEPS if step[0] and step[1])


def bond_list():
    reach = range(-HORIZON, HORIZON + 1)
    return [
        (x, y, z)
        for y in reach
        for x in reach
        for z in reach
        if 0 < x * x + y * y + z * z <= HORIZON * HORIZON
    ]


def bond_types(oz):
    kinds = {}
    for bond in bond_list():
        if bond[2] == oz:
            kinds.setdefault(tuple(sorted(map(abs, bond))), []).append(bond)
    return kinds


def influence(square):
    return (1.0 - square / (HORIZON * HORIZON)) ** 2


AWAY = tuple(oz for oz in range(-HORIZON, HORIZON + 1) if oz)


def moved(value, step):
    return pltpu.roll(value, (-step) % LANES, 1) if step else value


def inside(lane, step):
    return lane < LANES - step if step > 0 else lane >= -step


def middle_row(rows, index):
    return lax.rem(index + HORIZON, rows)


def within(rows, side=0):
    return [bond for bond in bond_list() if abs(bond[1]) <= rows and side * bond[0] <= 0]


MIDDLE = within(HORIZON - 1)
LEFT = within(HORIZON - 1, -1)
RIGHT = within(HORIZON - 1, 1)
BESIDE = within(HORIZON - 2)


def bond_scale(kind):
    square = sum(a * a for a in kind)
    length = math.sqrt(square)
    scale = 0.5 if sum(a > 0 for a in kind) == 1 else length / (2.0 * math.gcd(*kind))
    return STIFF * influence(square) * scale, length


def stretch_tile(vol_ext, ext, mine, known, bonds, y, slot, tile):
    start = pl.multiple_of(tile * SUB, SUB)
    row = y + HORIZON
    own = {}
    for index, bond in enumerate(bonds):
        ox, oy, oz = bond
        at = pl.ds(start + (SUB + ox), SUB)
        apart = []
        for k in range(3):
            if (k, oz) not in own:
                if oz:
                    own[k, oz] = mine[k, AWAY.index(oz), y, pl.ds(start + SUB, SUB), :]
                else:
                    own[k, oz] = ext[k, row, pl.ds(start + SUB, SUB), :]
            apart.append(ext[k, row + oy, at, :] - own[k, oz])
        squared = apart[0] * apart[0] + apart[1] * apart[1] + apart[2] * apart[2]
        scale, length = bond_scale(tuple(sorted(map(abs, bond))))
        pull = scale / length - scale * lax.rsqrt(squared)
        pull = pull * vol_ext[row + HORIZON + oy, at, :]
        for k in range(3):
            known[slot, index, k] = pull * apart[k]


def force_tile(vol_ext, ext, mine, sums, y, slot, tile, known=None, stored=(), place=None):
    start = pl.multiple_of(tile * SUB, SUB)
    row = y + HORIZON

    def load(field, ox, oy):
        at = pl.ds(start + (SUB + ox), SUB)
        if field == 6:
            return vol_ext[row + HORIZON + oy, at, :]
        return ext[field, row + oy, at, :]

    for oz in sorted(range(-HORIZON, HORIZON + 1), key=abs):
        kinds = bond_types(oz)
        own = {}
        for f in range(6):
            if oz == 0:
                own[f] = load(f, 0, 0)
            elif f < 3 or f == 5 or abs(oz) < HORIZON:
                own[f] = mine[f, AWAY.index(oz), y, pl.ds(start + SUB, SUB), :]
        summed = [None, None, None]

        def add(sums, factor, values):
            for k in range(3):
                term = factor * values[k]
                sums[k] = term if sums[k] is None else sums[k] + term

        for kind, bonds in kinds.items():
            scale, length = bond_scale(kind)
            common = math.gcd(*kind)
            count = sum(a > 0 for a in kind)
            fresh = [bond for bond in bonds if bond not in stored]
            late = len(fresh) > 6
            total = [None, None, None]
            for bond in bonds:
                ox, oy, _ = bond
                near = [k for k in range(3) if bond[k]]
                pair = {k: own[3 + k] + load(3 + k, ox, oy) for k in near}
                if count == 1:
                    ratio = pair[near[0]]
                else:
                    two = {k: pair[k] * pair[k] for k in near}
                    part = {k: (bond[k] // common) ** 2 for k in near}
                    if count == 2:
                        a, b = near
                        first = two[b] if part[a] == 1 else two[b] * float(part[a])
                        second = two[a] if part[b] == 1 else two[a] * float(part[b])
                        ratio = pair[a] * pair[b] * lax.rsqrt(first + second)
                    else:
                        odd = next(
                            k for k in near if sum(part[j] == part[k] for j in near) in (1, 3)
                        )
                        a, b = [k for k in near if k != odd]
                        first = two[a] * two[b]
                        if part[odd] != 1:
                            first = first * float(part[odd])
                        second = two[odd] * (two[a] + two[b])
                        if part[a] != 1:
                            second = second * float(part[a])
                        ratio = pair[a] * pair[b] * pair[odd] * lax.rsqrt(first + second)
                if bond in stored:
                    index = stored.index(bond)
                    add(summed, ratio, [known[place, index, k] for k in range(3)])
                    continue
                apart = [load(k, ox, oy) - own[k] for k in range(3)]
                squared = apart[0] * apart[0] + apart[1] * apart[1] + apart[2] * apart[2]
                if late:
                    pull = 1.0 / length - lax.rsqrt(squared)
                else:
                    pull = scale / length - scale * lax.rsqrt(squared)
                factor = (ratio * pull) * load(6, ox, oy)
                add(total if late else summed, factor, apart)
            if late:
                add(summed, scale, total)
        for k in range(3):
            sums[k, oz + HORIZON, slot, pl.ds(start, SUB), :] = summed[k]


def finish_row(vol_ext, parts, slot, y, force, at_row):
    lane = lax.broadcasted_iota(jnp.int32, (SUB, LANES), 1)
    for at in range(0, force.shape[2], SUB):
        alive = vol_ext[y + WIDE, SUB + at : 2 * SUB + at, :] > 0
        for k in range(3):
            total = parts[k, HORIZON, slot, at : at + SUB, :]
            for oz in AWAY:
                part = moved(parts[k, oz + HORIZON, slot, at : at + SUB, :], oz)
                total = total + jnp.where(inside(lane, oz), part, 0.0)
            force[k, at_row, at : at + SUB, :] = jnp.where(alive, total, 0.0)


def kernel(
    disp_in, volume_in, material_in, layers_in, vol_ext, ext, mine, first_force,
    known, known_left, known_right, known_beside,
    sums, disp, volume, material, layers,
    send_xv, send_cn, send_cf, send_x, send_c, got_xv, got_cn, got_cf, got_y, got_x, got_c,
    via_xv, via_x, sems, via_sems, load_sems,
):
    rows, cols = volume.shape[0], volume.shape[1]
    left = SUB
    right = left + cols
    bottom = WIDE + rows
    gx, gy = lax.axis_index("gx"), lax.axis_index("gy")
    nx, ny = lax.axis_size("gx"), lax.axis_size("gy")

    def has(step):
        dx, dy = step
        found = None
        for delta, at, size in ((dx, gx, nx), (dy, gy, ny)):
            if delta:
                test = at > 0 if delta < 0 else at < size - 1
                found = test if found is None else found & test
        return found

    odd = lax.rem(gy, 2)
    toward = 1 - 2 * odd
    paired = (gy + toward >= 0) & (gy + toward < ny)

    def to_partner(dy):
        return odd == (1 if dy < 0 else 0)

    def direct(step):
        if step in CORNERS:
            return has(step) & jnp.logical_not(to_partner(step[1]))
        return has(step)

    def device(step):
        return {"gx": gx + step[0], "gy": gy + step[1]}

    barrier = pltpu.get_barrier_semaphore()
    for step in STEPS:

        @pl.when(direct(step))
        def _():
            pl.semaphore_signal(barrier, inc=1, device_id=device(step), device_id_type=MESH)

    loads = [
        pltpu.make_async_copy(source, target, load_sems.at[index])
        for index, (source, target) in enumerate(
            ((material_in, material), (layers_in, layers), (volume_in, volume), (disp_in, disp))
        )
    ]
    for copy in loads:
        copy.start()

    lane = lax.broadcasted_iota(jnp.int32, (SUB, LANES), 1)
    sub_f = lax.broadcasted_iota(jnp.int32, (SUB, LANES), 0).astype(jnp.float32)
    zero = jnp.zeros((SUB, LANES), jnp.float32)

    def clear(ref, *where):
        ref[where] = jnp.zeros(ref.at[where].shape, jnp.float32)

    @pl.when(gy == 0)
    def _():
        clear(vol_ext, slice(0, WIDE), slice(left, right))
        clear(got_y, 0)

    @pl.when(gy == ny - 1)
    def _():
        clear(vol_ext, slice(bottom, bottom + WIDE), slice(left, right))
        clear(got_y, 1)

    for side, delta in enumerate(SIDES):

        @pl.when(jnp.logical_not(has((delta, 0))))
        def _():
            clear(got_xv, side)
            clear(got_x, side)

        @pl.when(jnp.logical_not(has((delta, 0)) & paired))
        def _():
            clear(via_xv, side)
            clear(via_x, side)

    for index, step in enumerate(CORNERS):

        @pl.when(jnp.logical_not(has(step)))
        def _():
            clear(got_cn, index)
            clear(got_cf, index)
            clear(got_c, index)

    for copy in loads[:3]:
        copy.wait()
    eye_row = lax.broadcasted_iota(jnp.int32, (cols, cols), 0)
    eye_col = lax.broadcasted_iota(jnp.int32, (cols, cols), 1)
    level = lax.broadcasted_iota(jnp.int32, (cols, LANES), 1).astype(jnp.float32)
    filled = jnp.where(material[...] > 0, layers[...], 0).astype(jnp.float32)
    for y in range(rows):
        line = jnp.broadcast_to(filled[y : y + 1, :], (cols, cols))
        top = jnp.sum(jnp.where(eye_row == eye_col, line, 0.0), axis=1, keepdims=True)
        vol_ext[WIDE + y, left:right, :] = jnp.where(
            level < jnp.broadcast_to(top, (cols, LANES)), volume[y], 0.0
        )

    def near_row(dy):
        return WIDE if dy < 0 else bottom - HORIZON

    def far_row(dy):
        return WIDE + HORIZON if dy < 0 else bottom - WIDE

    def near_halo(dy):
        return HORIZON if dy < 0 else bottom

    def far_halo(dy):
        return 0 if dy < 0 else bottom + HORIZON

    loads[3].wait()
    for side, delta in enumerate(SIDES):
        first = left if delta < 0 else right - WIDE
        for y in range(rows):
            send_xv[side, y * WIDE : (y + 1) * WIDE, :] = vol_ext[WIDE + y, first : first + WIDE, :]
        first = 0 if delta < 0 else cols - HORIZON
        for k in range(3):
            for y in range(rows):
                at = (k * rows + y) * HORIZON
                send_x[side, at : at + HORIZON, :] = disp[k, y, first : first + HORIZON, :]
    for index, (dx, dy) in enumerate(CORNERS):
        first = left if dx < 0 else right - WIDE
        for buffer, start in ((send_cn, near_row(dy)), (send_cf, far_row(dy))):
            for y in range(HORIZON):
                at = y * WIDE
                buffer[index, at : at + WIDE, :] = vol_ext[start + y, first : first + WIDE, :]
        first = 0 if dx < 0 else cols - HORIZON
        start = 0 if dy < 0 else rows - HORIZON
        for k in range(3):
            for y in range(HORIZON):
                at = (k * HORIZON + y) * HORIZON
                send_c[index, at : at + HORIZON, :] = disp[k, start + y, first : first + HORIZON, :]

    middle_x = left + cols // 2
    middle_y = HORIZON + rows // 2

    def place(k, value, y, at):
        width = value.shape[0]
        if k == 0:
            value = value + (sub_f[:width] + float(at - middle_x))
        if k == 1:
            value = value + (y - middle_y).astype(jnp.float32)
        ext[k, y, at : at + width, :] = value

    def own_row(y, carry):
        for at in range(0, cols, SUB):
            for k in range(3):
                place(k, disp[k, y, at : at + SUB, :], y + HORIZON, left + at)
                value = ext[k, y + HORIZON, left + at : left + at + SUB, :]
                for oz in AWAY:
                    there = moved(value, -oz)
                    if k == 2:
                        there = there - float(oz)
                    mine[k, AWAY.index(oz), y, left + at : left + at + SUB, :] = there
        return carry

    lax.fori_loop(0, rows, own_row, 0)

    own_tiles = cols // SUB
    early = rows - 2 * HORIZON
    inner = own_tiles - 2

    def stretch_ends(i, carry):
        y = i + (HORIZON - 1)
        stretch_tile(vol_ext, ext, mine, known_left, LEFT, y, i, 0)
        stretch_tile(vol_ext, ext, mine, known_right, RIGHT, y, i, own_tiles - 1)
        return carry

    lax.fori_loop(0, early + 2, stretch_ends, 0)

    peers = sum(direct(step).astype(jnp.int32) for step in STEPS)
    pl.semaphore_wait(barrier, peers)

    def cut_from(delta, size, width):
        return {-1: (0, width), 0: (0, size), 1: (size - width, width)}[delta]

    def vol_copy(step):
        return rows_copy(step, near_row, near_halo, send_cn, got_cn, 0)

    def far_copy(step):
        return rows_copy(step, far_row, far_halo, send_cf, got_cf, 4)

    def rows_copy(step, own, halo, send_corner, got_corner, sem):
        dx, dy = step
        if dx == 0:
            source = vol_ext.at[own(dy) : own(dy) + HORIZON, left:right]
            target = vol_ext.at[halo(-dy) : halo(-dy) + HORIZON, left:right]
        elif dy == 0:
            source, target = send_xv.at[0 if dx < 0 else 1], got_xv.at[0 if dx > 0 else 1]
        else:
            source = send_corner.at[CORNERS.index(step)]
            target = got_corner.at[CORNERS.index((-dx, -dy))]
        return pltpu.make_async_remote_copy(
            src_ref=source,
            dst_ref=target,
            send_sem=sems.at[sem, STEPS.index(step)],
            recv_sem=sems.at[sem + 1, STEPS.index((-dx, -dy))],
            device_id=device(step),
            device_id_type=MESH,
        )

    def via_copy(kind, side):
        source, target = ((got_xv, via_xv), (got_x, via_x))[kind]
        return pltpu.make_async_remote_copy(
            src_ref=source.at[side],
            dst_ref=target.at[side],
            send_sem=via_sems.at[2 * kind, side],
            recv_sem=via_sems.at[2 * kind + 1, side],
            device_id={"gx": gx, "gy": gy + toward},
            device_id_type=MESH,
        )

    def hand_on(kind):
        for side, delta in enumerate(SIDES):

            @pl.when(has((delta, 0)) & paired)
            def _():
                via_copy(kind, side).start()

    def handed(kind):
        for side, delta in enumerate(SIDES):

            @pl.when(has((delta, 0)) & paired)
            def _():
                via_copy(kind, side).wait_recv()

    def disp_copy(step):
        dx, dy = step
        if dx == 0:
            y0, yn = cut_from(dy, rows, HORIZON)
            source, target = disp.at[:, y0 : y0 + yn], got_y.at[0 if dy > 0 else 1]
        elif dy == 0:
            source, target = send_x.at[0 if dx < 0 else 1], got_x.at[0 if dx > 0 else 1]
        else:
            source, target = send_c.at[CORNERS.index(step)], got_c.at[CORNERS.index((-dx, -dy))]
        return pltpu.make_async_remote_copy(
            src_ref=source,
            dst_ref=target,
            send_sem=sems.at[2, STEPS.index(step)],
            recv_sem=sems.at[3, STEPS.index((-dx, -dy))],
            device_id=device(step),
            device_id_type=MESH,
        )

    along_x = [step for step in STEPS if step[1] == 0]
    along_y = [step for step in STEPS if step[0] == 0]
    sends = [(vol_copy, step) for step in (*along_y, *along_x, *CORNERS)]
    sends += [(disp_copy, step) for step in along_x]
    sends += [(far_copy, step) for step in (*CORNERS, *along_y)]
    sends += [(disp_copy, step) for step in (*CORNERS, *along_y)]
    for make, step in sends:

        @pl.when(direct(step))
        def _():
            make(step).start()

    def arrived(make, step):
        @pl.when(direct(step))
        def _():
            dx, dy = step
            make((-dx, -dy)).wait_recv()

    def fill_corners(buffer, row_there, row_here):
        for index, (dx, dy) in enumerate(CORNERS):
            side = 0 if dx < 0 else 1
            first = left - WIDE if dx < 0 else right
            there, here = row_there(-dy) - WIDE, row_here(dy)

            @pl.when(to_partner(dy))
            def _():
                for y in range(HORIZON):
                    at = (there + y) * WIDE
                    vol_ext[here + y, first : first + WIDE, :] = via_xv[side, at : at + WIDE, :]

            @pl.when(jnp.logical_not(to_partner(dy)))
            def _():
                for y in range(HORIZON):
                    at = y * WIDE
                    vol_ext[here + y, first : first + WIDE, :] = buffer[index, at : at + WIDE, :]

    bulk = math.pi * HORIZON**4 / 30.0
    near_rows = ext.shape[1]
    near_tiles = -(-(cols + 2 * HORIZON) // SUB)

    def factor_tile(y, at):
        row = y + HORIZON
        beside = {}
        for ax in range(HORIZON + 1):
            for ay in range(HORIZON + 1):
                if ax * ax + ay * ay > HORIZON * HORIZON:
                    continue
                total = None
                for dy in sorted({ay, -ay}):
                    for dx in sorted({ax, -ax}):
                        term = vol_ext[row + dy, at + dx : at + dx + SUB, :]
                        total = term if total is None else total + term
                beside[ax, ay] = total
        energy = [None, None, None]
        for k in range(3):
            for az in range(HORIZON + 1):
                layer = None
                for (ax, ay), total in beside.items():
                    square = ax * ax + ay * ay + az * az
                    part = (ax, ay, az)[k]
                    if not 0 < square <= HORIZON * HORIZON or not part:
                        continue
                    term = (influence(square) * part**4 / math.sqrt(square) ** 3) * total
                    layer = term if layer is None else layer + term
                if layer is None:
                    continue
                if az:
                    ahead = jnp.where(inside(lane, az), moved(layer, az), 0.0)
                    layer = ahead + jnp.where(inside(lane, -az), moved(layer, -az), 0.0)
                energy[k] = layer if energy[k] is None else energy[k] + layer
        alive = vol_ext[row, at : at + SUB, :] > 0
        for k in range(3):
            safe = jnp.where(alive, energy[k], 1.0)
            ext[3 + k, y, at : at + SUB, :] = jnp.where(alive, bulk / safe, 1.0)

    def factor_rows(first, step, stride, count, tiles):
        def body(i, carry):
            for y in range(count):
                for tile in tiles:
                    factor_tile(i * stride + first + y * step, left - HORIZON + tile * SUB)
            return carry

        return body

    def factor_moved(tiles):
        def body(i, carry):
            for part in range(4):
                y = i * 4 + part
                for tile in tiles:
                    at = left + tile * SUB
                    for k in range(3):
                        value = ext[3 + k, y + HORIZON, at : at + SUB, :]
                        for oz in AWAY:
                            if k == 2 or abs(oz) < HORIZON:
                                there = moved(value, -oz)
                                mine[3 + k, AWAY.index(oz), y, at : at + SUB, :] = there
            return carry

        return body

    def own_factors(near, own):
        lax.fori_loop(0, rows // 4, factor_rows(HORIZON, 1, 4, 4, near), 0)
        lax.fori_loop(0, rows // 4, factor_moved(own), 0)

    def middle():
        for step in along_y:
            arrived(vol_copy, step)
        own_factors(range(1, near_tiles - 1), range(1, own_tiles - 1))

    def edges():
        for step in along_x:
            arrived(vol_copy, step)
        hand_on(0)
        for side in range(2):
            first = left - WIDE if side == 0 else right
            for y in range(rows):
                at = y * WIDE
                vol_ext[WIDE + y, first : first + WIDE, :] = got_xv[side, at : at + WIDE, :]
        for step in CORNERS:
            arrived(vol_copy, step)
        handed(0)
        fill_corners(got_cn, near_row, near_halo)
        own_factors((0, near_tiles - 1), (0, own_tiles - 1))
        for step in along_x:
            arrived(disp_copy, step)
        hand_on(1)
        for side, at in ((0, left - HORIZON), (1, right)):

            def edge_row(y, carry):
                for k in range(3):
                    value = got_x[side, pl.ds((k * rows + y) * HORIZON, HORIZON), :]
                    place(k, value, y + HORIZON, at)
                return carry

            lax.fori_loop(0, rows, edge_row, 0)

    def halo_rows(side):
        delta = SIDES[side]
        base = 0 if side == 0 else HORIZON + rows

        def halo_row(y, carry):
            row = y + base
            for k in range(3):
                for at in range(0, cols, SUB):
                    place(k, got_y[side, k, y, at : at + SUB, :], row, left + at)
                for dx, at in ((-1, left - HORIZON), (1, right)):
                    corner = CORNERS.index((dx, delta))
                    there = y if delta > 0 else y + (rows - HORIZON)

                    @pl.when(to_partner(delta))
                    def _():
                        from_via = pl.ds((k * rows + there) * HORIZON, HORIZON)
                        place(k, via_x[0 if dx < 0 else 1, from_via, :], row, at)

                    @pl.when(jnp.logical_not(to_partner(delta)))
                    def _():
                        from_corner = pl.ds((k * HORIZON + y) * HORIZON, HORIZON)
                        place(k, got_c[corner, from_corner, :], row, at)

            return carry

        lax.fori_loop(0, HORIZON, halo_row, 0)

    def stretch_middle(i, carry):
        y = lax.div(i, inner) + (HORIZON - 1)
        stretch_tile(vol_ext, ext, mine, known, MIDDLE, y, i, lax.rem(i, inner) + 1)
        return carry

    def stretch_beside(i, carry):
        y = (HORIZON - 2) + lax.div(i, inner) * (early + 3)
        stretch_tile(vol_ext, ext, mine, known_beside, BESIDE, y, i, lax.rem(i, inner) + 1)
        return carry

    def middle_step(i, carry):
        slot = lax.div(i, inner)
        tile = lax.rem(i, inner) + 1
        y = slot + HORIZON
        force_tile(vol_ext, ext, mine, sums, y, slot, tile, known, MIDDLE, i + inner)
        return carry

    def end_step(tile, terms, stored):
        def body(slot, carry):
            y = slot + HORIZON
            force_tile(vol_ext, ext, mine, sums, y, slot, tile, terms, stored, slot + 1)
            return carry

        return body

    lax.fori_loop(0, (early + 2) * inner, stretch_middle, 0)
    lax.fori_loop(0, 2 * inner, stretch_beside, 0)
    middle()
    lax.fori_loop(0, early * inner, middle_step, 0)
    edges()
    lax.fori_loop(0, early, end_step(0, known_left, LEFT), 0)
    lax.fori_loop(0, early, end_step(own_tiles - 1, known_right, RIGHT), 0)
    for step in (*CORNERS, *along_y):
        arrived(far_copy, step)
    fill_corners(got_cf, far_row, far_halo)
    lax.fori_loop(0, HORIZON, factor_rows(0, rows + HORIZON, 1, 2, range(near_tiles)), 0)
    for slot in range(early):
        finish_row(vol_ext, sums, slot, slot + HORIZON, first_force, slot)
    for step in (*CORNERS, *along_y):
        arrived(disp_copy, step)
    handed(1)
    for side in (1, 0):
        halo_rows(side)

    for make, step in sends:

        @pl.when(direct(step))
        def _():
            make(step).wait_send()

    for side, delta in enumerate(SIDES):

        @pl.when(has((delta, 0)) & paired)
        def _():
            for kind in range(2):
                via_copy(kind, side).wait_send()


def rest(
    vol_ext, ext, mine, first_force, known, known_left, known_right, known_beside,
    fac_out, force_out, sums, force, out_sems, fac_sem,
):
    rows, cols = force.shape[1], force.shape[2]
    own = ext.at[3:6, HORIZON : HORIZON + rows, SUB : SUB + cols]
    done = first_force.shape[1]
    starts = [
        pltpu.make_async_copy(own, fac_out, fac_sem.at[0]),
        pltpu.make_async_copy(
            first_force, force_out.at[:, HORIZON : HORIZON + done], fac_sem.at[1]
        ),
    ]
    for copy in starts:
        copy.start()
    count = sums.shape[2]
    half = count // 2
    tiles = cols // SUB
    inner = tiles - 2
    each = tiles + 2

    def out_copy(y):
        return pltpu.make_async_copy(force.at[:, y], force_out.at[:, y], out_sems.at[y])

    def middle_step(i, carry):
        end = lax.div(i, inner)
        tile = lax.rem(i, inner)
        y = jnp.where(end == 0, HORIZON + done, HORIZON - 1)
        place = jnp.where(end == 0, (done + 1) * inner, 0) + tile
        slot = end * (count - 1)
        force_tile(vol_ext, ext, mine, sums, y, slot, tile + 1, known, MIDDLE, place)
        return carry

    def end_step(tile, terms, stored):
        def body(end, carry):
            y = jnp.where(end == 0, HORIZON + done, HORIZON - 1)
            place = jnp.where(end == 0, done + 1, 0)
            slot = end * (count - 1)
            force_tile(vol_ext, ext, mine, sums, y, slot, tile, terms, stored, place)
            return carry

        return body

    def beside_step(i, carry):
        end = lax.div(i, inner)
        tile = lax.rem(i, inner)
        y = jnp.where(end == 0, HORIZON + done + 1, HORIZON - 2)
        place = jnp.where(end == 0, inner, 0) + tile
        slot = jnp.where(end == 0, 1, count - 2)
        force_tile(vol_ext, ext, mine, sums, y, slot, tile + 1, known_beside, BESIDE, place)
        return carry

    def group(part, carry):
        def step(j, last):
            i = part * each + j
            between = lax.rem(i + (tiles - 2), tiles)
            end = (i < 2) | (i >= 2 * each - 2)
            slot = lax.div(i + (tiles - 2), tiles) + 1
            tile = jnp.where(end, lax.rem(i, 2) * (tiles - 1), between)
            force_tile(vol_ext, ext, mine, sums, middle_row(rows, slot + done), slot, tile)
            return last

        lax.fori_loop(0, each, step, carry)
        for index in range(half):
            slot = part * half + index
            y = middle_row(rows, slot + done)
            finish_row(vol_ext, sums, slot, y, force, y)
            out_copy(y).start()
        return carry

    lax.fori_loop(0, 2 * inner, middle_step, 0)
    lax.fori_loop(0, 2, end_step(0, known_left, LEFT), 0)
    lax.fori_loop(0, 2, end_step(tiles - 1, known_right, RIGHT), 0)
    lax.fori_loop(0, 2 * inner, beside_step, 0)
    lax.fori_loop(0, 2, group, 0)
    for copy in starts:
        copy.wait()
    for index in range(count):
        out_copy((index + done + HORIZON) % rows).wait()


def shards(displacement, volume, material, layers):
    _, rows, cols, depth = displacement.shape
    wide_rows, wide_cols = rows + 2 * WIDE, cols + 2 * SUB
    near_rows = rows + 2 * HORIZON
    hbm = pl.BlockSpec(memory_space=pltpu.MemorySpace.HBM)
    result = jax.ShapeDtypeStruct((3, rows, cols, depth), jnp.float32)

    def whole(count):
        return -(-count // SUB) * SUB

    edge, corner = whole(3 * rows * HORIZON), whole(3 * HORIZON * HORIZON)
    edge_vol, corner_vol = whole(rows * WIDE), whole(HORIZON * WIDE)

    def scratch(*shape):
        return pltpu.VMEM(shape + (depth,), jnp.float32)

    def held(*shape):
        return pltpu.VMEM(shape + (depth,), jnp.float32)

    def pin(values, space):
        return [pltpu.with_memory_space_constraint(value, space) for value in values]

    vmem = pl.BlockSpec(memory_space=pltpu.VMEM)
    early = rows - 2 * HORIZON
    frames = 2 * HORIZON + 1
    state = pl.pallas_call(
        kernel,
        out_shape=(
            held(wide_rows, wide_cols),
            held(6, near_rows, wide_cols),
            held(6, len(AWAY), rows, wide_cols),
            held(3, early, cols),
            held((early + 2) * (cols // SUB - 2), len(MIDDLE), 3, SUB),
            held(early + 2, len(LEFT), 3, SUB),
            held(early + 2, len(RIGHT), 3, SUB),
            held(2 * (cols // SUB - 2), len(BESIDE), 3, SUB),
        ),
        in_specs=[hbm] * 4,
        out_specs=(vmem,) * 8,
        scratch_shapes=[
            scratch(3, frames, early, cols),
            scratch(3, rows, cols),
            scratch(rows, cols),
            pltpu.VMEM((rows, cols), jnp.int32),
            pltpu.VMEM((rows, cols), jnp.int32),
            scratch(2, edge_vol),
            scratch(4, corner_vol),
            scratch(4, corner_vol),
            scratch(2, edge),
            scratch(4, corner),
            scratch(2, edge_vol),
            scratch(4, corner_vol),
            scratch(4, corner_vol),
            scratch(2, 3, HORIZON, cols),
            scratch(2, edge),
            scratch(4, corner),
            scratch(2, edge_vol),
            scratch(2, edge),
            pltpu.SemaphoreType.DMA((6, len(STEPS))),
            pltpu.SemaphoreType.DMA((4, 2)),
            pltpu.SemaphoreType.DMA((4,)),
        ],
        compiler_params=pltpu.CompilerParams(
            collective_id=0, has_side_effects=True, vmem_limit_bytes=VMEM_LIMIT
        ),
        name="gather",
    )(*pin((displacement, volume, material, layers), pltpu.MemorySpace.HBM))
    return pl.pallas_call(
        rest,
        out_shape=(result, result),
        in_specs=[vmem] * 8,
        out_specs=(hbm, hbm),
        scratch_shapes=[
            scratch(3, frames, rows - early, cols),
            scratch(3, rows, cols),
            pltpu.SemaphoreType.DMA((rows,)),
            pltpu.SemaphoreType.DMA((2,)),
        ],
        compiler_params=pltpu.CompilerParams(vmem_limit_bytes=VMEM_LIMIT),
        name="rest",
    )(*pin(state, pltpu.MemorySpace.VMEM))


def solution(mesh):
    return jax.shard_map(
        shards,
        mesh=mesh,
        in_specs=(P(None, "gy", "gx", None), P("gy", "gx", None), P("gy", "gx"), P("gy", "gx")),
        out_specs=(P(None, "gy", "gx", None), P(None, "gy", "gx", None)),
        check_vma=False,
    )
```

```python
import math

import jax
import jax.numpy as jnp
from jax import lax
from jax.experimental import pallas as pl
from jax.experimental.pallas import tpu as pltpu
from jax.sharding import PartitionSpec as P

HORIZON = 3
STIFF = 5.0
WIDE = 2 * HORIZON
LANES = 128
VMEM_LIMIT = 16 * 2**20
SUB = 8
MESH = pl.DeviceIdType.MESH
SIDES = (-1, 1)
STEPS = tuple((dx, dy) for dy in (-1, 0, 1) for dx in (-1, 0, 1) if (dx, dy) != (0, 0))
CORNERS = tuple(step for step in STEPS if step[0] and step[1])


def bond_list():
    reach = range(-HORIZON, HORIZON + 1)
    return [
        (x, y, z)
        for y in reach
        for x in reach
        for z in reach
        if 0 < x * x + y * y + z * z <= HORIZON * HORIZON
    ]


def bond_types(oz):
    kinds = {}
    for bond in bond_list():
        if bond[2] == oz:
            kinds.setdefault(tuple(sorted(map(abs, bond))), []).append(bond)
    return kinds


def influence(square):
    return (1.0 - square / (HORIZON * HORIZON)) ** 2


AWAY = tuple(oz for oz in range(-HORIZON, HORIZON + 1) if oz)


def moved(value, step):
    return pltpu.roll(value, (-step) % LANES, 1) if step else value


def inside(lane, step):
    return lane < LANES - step if step > 0 else lane >= -step


def middle_row(rows, index):
    return lax.rem(index + HORIZON, rows)


def within(rows, side=0):
    return [bond for bond in bond_list() if abs(bond[1]) <= rows and side * bond[0] <= 0]


MIDDLE = within(HORIZON - 1)
LEFT = within(HORIZON - 1, -1)
RIGHT = within(HORIZON - 1, 1)
BESIDE = within(HORIZON - 2)


def bond_scale(kind):
    square = sum(a * a for a in kind)
    length = math.sqrt(square)
    scale = 0.5 if sum(a > 0 for a in kind) == 1 else length / (2.0 * math.gcd(*kind))
    return STIFF * influence(square) * scale, length


def stretch_tile(vol_ext, ext, mine, known, bonds, y, slot, tile):
    start = pl.multiple_of(tile * SUB, SUB)
    row = y + HORIZON
    own = {}
    for index, bond in enumerate(bonds):
        ox, oy, oz = bond
        at = pl.ds(start + (SUB + ox), SUB)
        apart = []
        for k in range(3):
            if (k, oz) not in own:
                if oz:
                    own[k, oz] = mine[k, AWAY.index(oz), y, pl.ds(start + SUB, SUB), :]
                else:
                    own[k, oz] = ext[k, row, pl.ds(start + SUB, SUB), :]
            apart.append(ext[k, row + oy, at, :] - own[k, oz])
        squared = apart[0] * apart[0] + apart[1] * apart[1] + apart[2] * apart[2]
        scale, length = bond_scale(tuple(sorted(map(abs, bond))))
        pull = scale / length - scale * lax.rsqrt(squared)
        pull = pull * vol_ext[row + HORIZON + oy, at, :]
        for k in range(3):
            known[slot, index, k] = pull * apart[k]


def force_tile(vol_ext, ext, mine, sums, y, slot, tile, known=None, stored=(), place=None):
    start = pl.multiple_of(tile * SUB, SUB)
    row = y + HORIZON

    def load(field, ox, oy):
        at = pl.ds(start + (SUB + ox), SUB)
        if field == 6:
            return vol_ext[row + HORIZON + oy, at, :]
        return ext[field, row + oy, at, :]

    for oz in sorted(range(-HORIZON, HORIZON + 1), key=abs):
        kinds = bond_types(oz)
        own = {}
        for f in range(6):
            if oz == 0:
                own[f] = load(f, 0, 0)
            elif f < 3 or f == 5 or abs(oz) < HORIZON:
                own[f] = mine[f, AWAY.index(oz), y, pl.ds(start + SUB, SUB), :]
        summed = [None, None, None]

        def add(sums, factor, values):
            for k in range(3):
                term = factor * values[k]
                sums[k] = term if sums[k] is None else sums[k] + term

        for kind, bonds in kinds.items():
            scale, length = bond_scale(kind)
            common = math.gcd(*kind)
            count = sum(a > 0 for a in kind)
            fresh = [bond for bond in bonds if bond not in stored]
            late = len(fresh) > 6
            total = [None, None, None]
            for bond in bonds:
                ox, oy, _ = bond
                near = [k for k in range(3) if bond[k]]
                pair = {k: own[3 + k] + load(3 + k, ox, oy) for k in near}
                if count == 1:
                    ratio = pair[near[0]]
                else:
                    two = {k: pair[k] * pair[k] for k in near}
                    part = {k: (bond[k] // common) ** 2 for k in near}
                    if count == 2:
                        a, b = near
                        first = two[b] if part[a] == 1 else two[b] * float(part[a])
                        second = two[a] if part[b] == 1 else two[a] * float(part[b])
                        ratio = pair[a] * pair[b] * lax.rsqrt(first + second)
                    else:
                        odd = next(
                            k for k in near if sum(part[j] == part[k] for j in near) in (1, 3)
                        )
                        a, b = [k for k in near if k != odd]
                        first = two[a] * two[b]
                        if part[odd] != 1:
                            first = first * float(part[odd])
                        second = two[odd] * (two[a] + two[b])
                        if part[a] != 1:
                            second = second * float(part[a])
                        ratio = pair[a] * pair[b] * pair[odd] * lax.rsqrt(first + second)
                if bond in stored:
                    index = stored.index(bond)
                    add(summed, ratio, [known[place, index, k] for k in range(3)])
                    continue
                apart = [load(k, ox, oy) - own[k] for k in range(3)]
                squared = apart[0] * apart[0] + apart[1] * apart[1] + apart[2] * apart[2]
                if late:
                    pull = 1.0 / length - lax.rsqrt(squared)
                else:
                    pull = scale / length - scale * lax.rsqrt(squared)
                factor = (ratio * pull) * load(6, ox, oy)
                add(total if late else summed, factor, apart)
            if late:
                add(summed, scale, total)
        for k in range(3):
            sums[k, oz + HORIZON, slot, pl.ds(start, SUB), :] = summed[k]


def finish_row(vol_ext, parts, slot, y, force, at_row):
    lane = lax.broadcasted_iota(jnp.int32, (SUB, LANES), 1)
    for at in range(0, force.shape[2], SUB):
        alive = vol_ext[y + WIDE, SUB + at : 2 * SUB + at, :] > 0
        for k in range(3):
            total = parts[k, HORIZON, slot, at : at + SUB, :]
            for oz in AWAY:
                part = moved(parts[k, oz + HORIZON, slot, at : at + SUB, :], oz)
                total = total + jnp.where(inside(lane, oz), part, 0.0)
            force[k, at_row, at : at + SUB, :] = jnp.where(alive, total, 0.0)


def kernel(
    disp_in, volume_in, material_in, layers_in, vol_ext, ext, mine, first_force,
    known, known_left, known_right, known_beside,
    sums, disp, volume, material, layers,
    send_xv, send_cn, send_cf, send_x, send_c, got_xv, got_cn, got_cf, got_y, got_x, got_c,
    via_xv, via_x, sems, via_sems, load_sems,
):
    rows, cols = volume.shape[0], volume.shape[1]
    left = SUB
    right = left + cols
    bottom = WIDE + rows
    gx, gy = lax.axis_index("gx"), lax.axis_index("gy")
    nx, ny = lax.axis_size("gx"), lax.axis_size("gy")

    def has(step):
        dx, dy = step
        found = None
        for delta, at, size in ((dx, gx, nx), (dy, gy, ny)):
            if delta:
                test = at > 0 if delta < 0 else at < size - 1
                found = test if found is None else found & test
        return found

    odd = lax.rem(gy, 2)
    toward = 1 - 2 * odd
    paired = (gy + toward >= 0) & (gy + toward < ny)

    def to_partner(dy):
        return odd == (1 if dy < 0 else 0)

    def direct(step):
        if step in CORNERS:
            return has(step) & jnp.logical_not(to_partner(step[1]))
        return has(step)

    def device(step):
        return {"gx": gx + step[0], "gy": gy + step[1]}

    barrier = pltpu.get_barrier_semaphore()
    for step in STEPS:

        @pl.when(direct(step))
        def _():
            pl.semaphore_signal(barrier, inc=1, device_id=device(step), device_id_type=MESH)

    loads = [
        pltpu.make_async_copy(source, target, load_sems.at[index])
        for index, (source, target) in enumerate(
            ((material_in, material), (layers_in, layers), (volume_in, volume), (disp_in, disp))
        )
    ]
    for copy in loads:
        copy.start()

    lane = lax.broadcasted_iota(jnp.int32, (SUB, LANES), 1)
    sub_f = lax.broadcasted_iota(jnp.int32, (SUB, LANES), 0).astype(jnp.float32)
    zero = jnp.zeros((SUB, LANES), jnp.float32)

    def clear(ref, *where):
        ref[where] = jnp.zeros(ref.at[where].shape, jnp.float32)

    @pl.when(gy == 0)
    def _():
        clear(vol_ext, slice(0, WIDE), slice(left, right))
        clear(got_y, 0)

    @pl.when(gy == ny - 1)
    def _():
        clear(vol_ext, slice(bottom, bottom + WIDE), slice(left, right))
        clear(got_y, 1)

    for side, delta in enumerate(SIDES):

        @pl.when(jnp.logical_not(has((delta, 0))))
        def _():
            clear(got_xv, side)
            clear(got_x, side)

        @pl.when(jnp.logical_not(has((delta, 0)) & paired))
        def _():
            clear(via_xv, side)
            clear(via_x, side)

    for index, step in enumerate(CORNERS):

        @pl.when(jnp.logical_not(has(step)))
        def _():
            clear(got_cn, index)
            clear(got_cf, index)
            clear(got_c, index)

    for copy in loads[:3]:
        copy.wait()
    eye_row = lax.broadcasted_iota(jnp.int32, (cols, cols), 0)
    eye_col = lax.broadcasted_iota(jnp.int32, (cols, cols), 1)
    level = lax.broadcasted_iota(jnp.int32, (cols, LANES), 1).astype(jnp.float32)
    filled = jnp.where(material[...] > 0, layers[...], 0).astype(jnp.float32)
    for y in range(rows):
        line = jnp.broadcast_to(filled[y : y + 1, :], (cols, cols))
        top = jnp.sum(jnp.where(eye_row == eye_col, line, 0.0), axis=1, keepdims=True)
        vol_ext[WIDE + y, left:right, :] = jnp.where(
            level < jnp.broadcast_to(top, (cols, LANES)), volume[y], 0.0
        )

    def near_row(dy):
        return WIDE if dy < 0 else bottom - HORIZON

    def far_row(dy):
        return WIDE + HORIZON if dy < 0 else bottom - WIDE

    def near_halo(dy):
        return HORIZON if dy < 0 else bottom

    def far_halo(dy):
        return 0 if dy < 0 else bottom + HORIZON

    loads[3].wait()
    for side, delta in enumerate(SIDES):
        first = left if delta < 0 else right - WIDE
        for y in range(rows):
            send_xv[side, y * WIDE : (y + 1) * WIDE, :] = vol_ext[WIDE + y, first : first + WIDE, :]
        first = 0 if delta < 0 else cols - HORIZON
        for k in range(3):
            for y in range(rows):
                at = (k * rows + y) * HORIZON
                send_x[side, at : at + HORIZON, :] = disp[k, y, first : first + HORIZON, :]
    for index, (dx, dy) in enumerate(CORNERS):
        first = left if dx < 0 else right - WIDE
        for buffer, start in ((send_cn, near_row(dy)), (send_cf, far_row(dy))):
            for y in range(HORIZON):
                at = y * WIDE
                buffer[index, at : at + WIDE, :] = vol_ext[start + y, first : first + WIDE, :]
        first = 0 if dx < 0 else cols - HORIZON
        start = 0 if dy < 0 else rows - HORIZON
        for k in range(3):
            for y in range(HORIZON):
                at = (k * HORIZON + y) * HORIZON
                send_c[index, at : at + HORIZON, :] = disp[k, start + y, first : first + HORIZON, :]

    middle_x = left + cols // 2
    middle_y = HORIZON + rows // 2

    def place(k, value, y, at):
        width = value.shape[0]
        if k == 0:
            value = value + (sub_f[:width] + float(at - middle_x))
        if k == 1:
            value = value + (y - middle_y).astype(jnp.float32)
        ext[k, y, at : at + width, :] = value

    def own_row(y, carry):
        for at in range(0, cols, SUB):
            for k in range(3):
                place(k, disp[k, y, at : at + SUB, :], y + HORIZON, left + at)
                value = ext[k, y + HORIZON, left + at : left + at + SUB, :]
                for oz in AWAY:
                    there = moved(value, -oz)
                    if k == 2:
                        there = there - float(oz)
                    mine[k, AWAY.index(oz), y, left + at : left + at + SUB, :] = there
        return carry

    lax.fori_loop(0, rows, own_row, 0)

    own_tiles = cols // SUB
    early = rows - 2 * HORIZON
    inner = own_tiles - 2

    def stretch_ends(i, carry):
        y = i + (HORIZON - 1)
        stretch_tile(vol_ext, ext, mine, known_left, LEFT, y, i, 0)
        stretch_tile(vol_ext, ext, mine, known_right, RIGHT, y, i, own_tiles - 1)
        return carry


    peers = sum(direct(step).astype(jnp.int32) for step in STEPS)
    pl.semaphore_wait(barrier, peers)

    def cut_from(delta, size, width):
        return {-1: (0, width), 0: (0, size), 1: (size - width, width)}[delta]

    def vol_copy(step):
        return rows_copy(step, near_row, near_halo, send_cn, got_cn, 0)

    def far_copy(step):
        return rows_copy(step, far_row, far_halo, send_cf, got_cf, 4)

    def rows_copy(step, own, halo, send_corner, got_corner, sem):
        dx, dy = step
        if dx == 0:
            source = vol_ext.at[own(dy) : own(dy) + HORIZON, left:right]
            target = vol_ext.at[halo(-dy) : halo(-dy) + HORIZON, left:right]
        elif dy == 0:
            source, target = send_xv.at[0 if dx < 0 else 1], got_xv.at[0 if dx > 0 else 1]
        else:
            source = send_corner.at[CORNERS.index(step)]
            target = got_corner.at[CORNERS.index((-dx, -dy))]
        return pltpu.make_async_remote_copy(
            src_ref=source,
            dst_ref=target,
            send_sem=sems.at[sem, STEPS.index(step)],
            recv_sem=sems.at[sem + 1, STEPS.index((-dx, -dy))],
            device_id=device(step),
            device_id_type=MESH,
        )

    def via_copy(kind, side):
        source, target = ((got_xv, via_xv), (got_x, via_x))[kind]
        return pltpu.make_async_remote_copy(
            src_ref=source.at[side],
            dst_ref=target.at[side],
            send_sem=via_sems.at[2 * kind, side],
            recv_sem=via_sems.at[2 * kind + 1, side],
            device_id={"gx": gx, "gy": gy + toward},
            device_id_type=MESH,
        )

    def hand_on(kind):
        for side, delta in enumerate(SIDES):

            @pl.when(has((delta, 0)) & paired)
            def _():
                via_copy(kind, side).start()

    def handed(kind):
        for side, delta in enumerate(SIDES):

            @pl.when(has((delta, 0)) & paired)
            def _():
                via_copy(kind, side).wait_recv()

    def disp_copy(step):
        dx, dy = step
        if dx == 0:
            y0, yn = cut_from(dy, rows, HORIZON)
            source, target = disp.at[:, y0 : y0 + yn], got_y.at[0 if dy > 0 else 1]
        elif dy == 0:
            source, target = send_x.at[0 if dx < 0 else 1], got_x.at[0 if dx > 0 else 1]
        else:
            source, target = send_c.at[CORNERS.index(step)], got_c.at[CORNERS.index((-dx, -dy))]
        return pltpu.make_async_remote_copy(
            src_ref=source,
            dst_ref=target,
            send_sem=sems.at[2, STEPS.index(step)],
            recv_sem=sems.at[3, STEPS.index((-dx, -dy))],
            device_id=device(step),
            device_id_type=MESH,
        )

    along_x = [step for step in STEPS if step[1] == 0]
    along_y = [step for step in STEPS if step[0] == 0]
    sends = [(vol_copy, step) for step in (*along_y, *along_x, *CORNERS)]
    sends += [(disp_copy, step) for step in along_x]
    sends += [(far_copy, step) for step in (*CORNERS, *along_y)]
    sends += [(disp_copy, step) for step in (*CORNERS, *along_y)]
    for make, step in sends:

        @pl.when(direct(step))
        def _():
            make(step).start()

    def arrived(make, step):
        @pl.when(direct(step))
        def _():
            dx, dy = step
            make((-dx, -dy)).wait_recv()

    def fill_corners(buffer, row_there, row_here):
        for index, (dx, dy) in enumerate(CORNERS):
            side = 0 if dx < 0 else 1
            first = left - WIDE if dx < 0 else right
            there, here = row_there(-dy) - WIDE, row_here(dy)

            @pl.when(to_partner(dy))
            def _():
                for y in range(HORIZON):
                    at = (there + y) * WIDE
                    vol_ext[here + y, first : first + WIDE, :] = via_xv[side, at : at + WIDE, :]

            @pl.when(jnp.logical_not(to_partner(dy)))
            def _():
                for y in range(HORIZON):
                    at = y * WIDE
                    vol_ext[here + y, first : first + WIDE, :] = buffer[index, at : at + WIDE, :]

    bulk = math.pi * HORIZON**4 / 30.0
    near_rows = ext.shape[1]
    near_tiles = -(-(cols + 2 * HORIZON) // SUB)

    def factor_tile(y, at):
        row = y + HORIZON
        beside = {}
        for ax in range(HORIZON + 1):
            for ay in range(HORIZON + 1):
                if ax * ax + ay * ay > HORIZON * HORIZON:
                    continue
                total = None
                for dy in sorted({ay, -ay}):
                    for dx in sorted({ax, -ax}):
                        term = vol_ext[row + dy, at + dx : at + dx + SUB, :]
                        total = term if total is None else total + term
                beside[ax, ay] = total
        energy = [None, None, None]
        for k in range(3):
            for az in range(HORIZON + 1):
                layer = None
                for (ax, ay), total in beside.items():
                    square = ax * ax + ay * ay + az * az
                    part = (ax, ay, az)[k]
                    if not 0 < square <= HORIZON * HORIZON or not part:
                        continue
                    term = (influence(square) * part**4 / math.sqrt(square) ** 3) * total
                    layer = term if layer is None else layer + term
                if layer is None:
                    continue
                if az:
                    ahead = jnp.where(inside(lane, az), moved(layer, az), 0.0)
                    layer = ahead + jnp.where(inside(lane, -az), moved(layer, -az), 0.0)
                energy[k] = layer if energy[k] is None else energy[k] + layer
        alive = vol_ext[row, at : at + SUB, :] > 0
        for k in range(3):
            safe = jnp.where(alive, energy[k], 1.0)
            ext[3 + k, y, at : at + SUB, :] = jnp.where(alive, bulk / safe, 1.0)

    def factor_rows(first, step, stride, count, tiles):
        def body(i, carry):
            for y in range(count):
                for tile in tiles:
                    factor_tile(i * stride + first + y * step, left - HORIZON + tile * SUB)
            return carry

        return body

    def factor_moved(tiles):
        def body(i, carry):
            for part in range(4):
                y = i * 4 + part
                for tile in tiles:
                    at = left + tile * SUB
                    for k in range(3):
                        value = ext[3 + k, y + HORIZON, at : at + SUB, :]
                        for oz in AWAY:
                            if k == 2 or abs(oz) < HORIZON:
                                there = moved(value, -oz)
                                mine[3 + k, AWAY.index(oz), y, at : at + SUB, :] = there
            return carry

        return body

    def own_factors(near, own):
        lax.fori_loop(0, rows // 4, factor_rows(HORIZON, 1, 4, 4, near), 0)
        lax.fori_loop(0, rows // 4, factor_moved(own), 0)

    def middle():
        for step in along_y:
            arrived(vol_copy, step)
        own_factors(range(1, near_tiles - 1), range(1, own_tiles - 1))

    def edges():
        for step in along_x:
            arrived(vol_copy, step)
        hand_on(0)
        for side in range(2):
            first = left - WIDE if side == 0 else right
            for y in range(rows):
                at = y * WIDE
                vol_ext[WIDE + y, first : first + WIDE, :] = got_xv[side, at : at + WIDE, :]
        for step in CORNERS:
            arrived(vol_copy, step)
        handed(0)
        fill_corners(got_cn, near_row, near_halo)
        own_factors((0, near_tiles - 1), (0, own_tiles - 1))
        for step in along_x:
            arrived(disp_copy, step)
        hand_on(1)
        for side, at in ((0, left - HORIZON), (1, right)):

            def edge_row(y, carry):
                for k in range(3):
                    value = got_x[side, pl.ds((k * rows + y) * HORIZON, HORIZON), :]
                    place(k, value, y + HORIZON, at)
                return carry

            lax.fori_loop(0, rows, edge_row, 0)

    def halo_rows(side):
        delta = SIDES[side]
        base = 0 if side == 0 else HORIZON + rows

        def halo_row(y, carry):
            row = y + base
            for k in range(3):
                for at in range(0, cols, SUB):
                    place(k, got_y[side, k, y, at : at + SUB, :], row, left + at)
                for dx, at in ((-1, left - HORIZON), (1, right)):
                    corner = CORNERS.index((dx, delta))
                    there = y if delta > 0 else y + (rows - HORIZON)

                    @pl.when(to_partner(delta))
                    def _():
                        from_via = pl.ds((k * rows + there) * HORIZON, HORIZON)
                        place(k, via_x[0 if dx < 0 else 1, from_via, :], row, at)

                    @pl.when(jnp.logical_not(to_partner(delta)))
                    def _():
                        from_corner = pl.ds((k * HORIZON + y) * HORIZON, HORIZON)
                        place(k, got_c[corner, from_corner, :], row, at)

            return carry

        lax.fori_loop(0, HORIZON, halo_row, 0)

    def stretch_middle(i, carry):
        y = lax.div(i, inner) + (HORIZON - 1)
        stretch_tile(vol_ext, ext, mine, known, MIDDLE, y, i, lax.rem(i, inner) + 1)
        return carry

    def stretch_beside(i, carry):
        y = (HORIZON - 2) + lax.div(i, inner) * (early + 3)
        stretch_tile(vol_ext, ext, mine, known_beside, BESIDE, y, i, lax.rem(i, inner) + 1)
        return carry

    def middle_step(i, carry):
        slot = lax.div(i, inner)
        tile = lax.rem(i, inner) + 1
        y = slot + HORIZON
        force_tile(vol_ext, ext, mine, sums, y, slot, tile, known, MIDDLE, i + inner)
        return carry

    def end_step(tile, terms, stored):
        def body(slot, carry):
            y = slot + HORIZON
            force_tile(vol_ext, ext, mine, sums, y, slot, tile, terms, stored, slot + 1)
            return carry

        return body

    lax.fori_loop(0, early + 2, stretch_ends, 0)
    lax.fori_loop(0, (early + 2) * inner, stretch_middle, 0)
    lax.fori_loop(0, 2 * inner, stretch_beside, 0)
    middle()
    lax.fori_loop(0, early * inner, middle_step, 0)
    edges()
    lax.fori_loop(0, early, end_step(0, known_left, LEFT), 0)
    lax.fori_loop(0, early, end_step(own_tiles - 1, known_right, RIGHT), 0)
    for step in (*CORNERS, *along_y):
        arrived(far_copy, step)
    fill_corners(got_cf, far_row, far_halo)
    lax.fori_loop(0, HORIZON, factor_rows(0, rows + HORIZON, 1, 2, range(near_tiles)), 0)
    for slot in range(early):
        finish_row(vol_ext, sums, slot, slot + HORIZON, first_force, slot)
    for step in (*CORNERS, *along_y):
        arrived(disp_copy, step)
    handed(1)
    for side in (1, 0):
        halo_rows(side)

    for make, step in sends:

        @pl.when(direct(step))
        def _():
            make(step).wait_send()

    for side, delta in enumerate(SIDES):

        @pl.when(has((delta, 0)) & paired)
        def _():
            for kind in range(2):
                via_copy(kind, side).wait_send()


def rest(
    vol_ext, ext, mine, first_force, known, known_left, known_right, known_beside,
    fac_out, force_out, sums, force, out_sems, fac_sem,
):
    rows, cols = force.shape[1], force.shape[2]
    own = ext.at[3:6, HORIZON : HORIZON + rows, SUB : SUB + cols]
    done = first_force.shape[1]
    starts = [
        pltpu.make_async_copy(own, fac_out, fac_sem.at[0]),
        pltpu.make_async_copy(
            first_force, force_out.at[:, HORIZON : HORIZON + done], fac_sem.at[1]
        ),
    ]
    for copy in starts:
        copy.start()
    count = sums.shape[2]
    half = count // 2
    tiles = cols // SUB
    inner = tiles - 2
    each = tiles + 2

    def out_copy(y):
        return pltpu.make_async_copy(force.at[:, y], force_out.at[:, y], out_sems.at[y])

    def middle_step(i, carry):
        end = lax.div(i, inner)
        tile = lax.rem(i, inner)
        y = jnp.where(end == 0, HORIZON + done, HORIZON - 1)
        place = jnp.where(end == 0, (done + 1) * inner, 0) + tile
        slot = end * (count - 1)
        force_tile(vol_ext, ext, mine, sums, y, slot, tile + 1, known, MIDDLE, place)
        return carry

    def end_step(tile, terms, stored):
        def body(end, carry):
            y = jnp.where(end == 0, HORIZON + done, HORIZON - 1)
            place = jnp.where(end == 0, done + 1, 0)
            slot = end * (count - 1)
            force_tile(vol_ext, ext, mine, sums, y, slot, tile, terms, stored, place)
            return carry

        return body

    def beside_step(i, carry):
        end = lax.div(i, inner)
        tile = lax.rem(i, inner)
        y = jnp.where(end == 0, HORIZON + done + 1, HORIZON - 2)
        place = jnp.where(end == 0, inner, 0) + tile
        slot = jnp.where(end == 0, 1, count - 2)
        force_tile(vol_ext, ext, mine, sums, y, slot, tile + 1, known_beside, BESIDE, place)
        return carry

    def group(part, carry):
        def step(j, last):
            i = part * each + j
            between = lax.rem(i + (tiles - 2), tiles)
            end = (i < 2) | (i >= 2 * each - 2)
            slot = lax.div(i + (tiles - 2), tiles) + 1
            tile = jnp.where(end, lax.rem(i, 2) * (tiles - 1), between)
            force_tile(vol_ext, ext, mine, sums, middle_row(rows, slot + done), slot, tile)
            return last

        lax.fori_loop(0, each, step, carry)
        for index in range(half):
            slot = part * half + index
            y = middle_row(rows, slot + done)
            finish_row(vol_ext, sums, slot, y, force, y)
            out_copy(y).start()
        return carry

    lax.fori_loop(0, 2 * inner, middle_step, 0)
    lax.fori_loop(0, 2, end_step(0, known_left, LEFT), 0)
    lax.fori_loop(0, 2, end_step(tiles - 1, known_right, RIGHT), 0)
    lax.fori_loop(0, 2 * inner, beside_step, 0)
    lax.fori_loop(0, 2, group, 0)
    for copy in starts:
        copy.wait()
    for index in range(count):
        out_copy((index + done + HORIZON) % rows).wait()


def shards(displacement, volume, material, layers):
    _, rows, cols, depth = displacement.shape
    wide_rows, wide_cols = rows + 2 * WIDE, cols + 2 * SUB
    near_rows = rows + 2 * HORIZON
    hbm = pl.BlockSpec(memory_space=pltpu.MemorySpace.HBM)
    result = jax.ShapeDtypeStruct((3, rows, cols, depth), jnp.float32)

    def whole(count):
        return -(-count // SUB) * SUB

    edge, corner = whole(3 * rows * HORIZON), whole(3 * HORIZON * HORIZON)
    edge_vol, corner_vol = whole(rows * WIDE), whole(HORIZON * WIDE)

    def scratch(*shape):
        return pltpu.VMEM(shape + (depth,), jnp.float32)

    def held(*shape):
        return pltpu.VMEM(shape + (depth,), jnp.float32)

    def pin(values, space):
        return [pltpu.with_memory_space_constraint(value, space) for value in values]

    vmem = pl.BlockSpec(memory_space=pltpu.VMEM)
    early = rows - 2 * HORIZON
    frames = 2 * HORIZON + 1
    state = pl.pallas_call(
        kernel,
        out_shape=(
            held(wide_rows, wide_cols),
            held(6, near_rows, wide_cols),
            held(6, len(AWAY), rows, wide_cols),
            held(3, early, cols),
            held((early + 2) * (cols // SUB - 2), len(MIDDLE), 3, SUB),
            held(early + 2, len(LEFT), 3, SUB),
            held(early + 2, len(RIGHT), 3, SUB),
            held(2 * (cols // SUB - 2), len(BESIDE), 3, SUB),
        ),
        in_specs=[hbm] * 4,
        out_specs=(vmem,) * 8,
        scratch_shapes=[
            scratch(3, frames, early, cols),
            scratch(3, rows, cols),
            scratch(rows, cols),
            pltpu.VMEM((rows, cols), jnp.int32),
            pltpu.VMEM((rows, cols), jnp.int32),
            scratch(2, edge_vol),
            scratch(4, corner_vol),
            scratch(4, corner_vol),
            scratch(2, edge),
            scratch(4, corner),
            scratch(2, edge_vol),
            scratch(4, corner_vol),
            scratch(4, corner_vol),
            scratch(2, 3, HORIZON, cols),
            scratch(2, edge),
            scratch(4, corner),
            scratch(2, edge_vol),
            scratch(2, edge),
            pltpu.SemaphoreType.DMA((6, len(STEPS))),
            pltpu.SemaphoreType.DMA((4, 2)),
            pltpu.SemaphoreType.DMA((4,)),
        ],
        compiler_params=pltpu.CompilerParams(
            collective_id=0, has_side_effects=True, vmem_limit_bytes=VMEM_LIMIT
        ),
        name="gather",
    )(*pin((displacement, volume, material, layers), pltpu.MemorySpace.HBM))
    return pl.pallas_call(
        rest,
        out_shape=(result, result),
        in_specs=[vmem] * 8,
        out_specs=(hbm, hbm),
        scratch_shapes=[
            scratch(3, frames, rows - early, cols),
            scratch(3, rows, cols),
            pltpu.SemaphoreType.DMA((rows,)),
            pltpu.SemaphoreType.DMA((2,)),
        ],
        compiler_params=pltpu.CompilerParams(vmem_limit_bytes=VMEM_LIMIT),
        name="rest",
    )(*pin(state, pltpu.MemorySpace.VMEM))


def solution(mesh):
    return jax.shard_map(
        shards,
        mesh=mesh,
        in_specs=(P(None, "gy", "gx", None), P("gy", "gx", None), P("gy", "gx"), P("gy", "gx")),
        out_specs=(P(None, "gy", "gx", None), P(None, "gy", "gx", None)),
        check_vma=False,
    )
```
